32 devices in a mesh: cell: 2 (over x), tm: 16 (over z, y, core).
Axes of the slice: x: 2, y: 2, z: 4, core: 2. Of those that a mesh axis runs over, the one named last changes fastest.
Arguments:
- readings: bfloat16 [128, 160, 256], P(('cell', 'tm')), may hold values from -24 to 24
- cell_ids: int32 [32, 256], P(('cell', 'tm')), may hold values from 0 to 255, each once within a row
- valid_days: int32 [32], replicated, may hold values from 1 to 4
Outputs:
- covariance: float32 [256, 25600], P(('cell', 'tm'))
The draws below stay inside these ranges and needn't reach their ends.
Inputs may be any that keep to these rules, and one draw needn't show every extreme that they name: Each row of cell_ids orders all 256 cells, each once. Slab s is observed on its first valid_days[s] days; its other days are missing.
All inputs are finite; a program needn't handle non-finite values.
Results may differ from the reference program's by a relative error of at most 0.0003.
Values may be sent and summed in bfloat16 or wider, within the bound.
A program may use at most 128 MiB of HBM per device.

```python
import math
import jax
import jax.numpy as jnp
from jax import lax

F = 160
DS = 4
GROUPS = 16
SLABS = 32
DAYS = 128
CPC = 128
CELLS = 256
N_CELL = 2


def draw_readings(key, part):
    keys = jax.random.split(jax.random.fold_in(key, 11), 5)
    day_group = jnp.arange(DAYS, dtype=jnp.int32) // DS % GROUPS
    spread = day_group.astype(jnp.float32) / max(GROUPS - 1, 1)
    ramp = 0.5 + spread
    feature_scale = jnp.exp(jax.random.uniform(keys[0], (F, 1), jnp.float32, math.log(0.5), math.log(2.0)))
    cell_scale = jnp.exp(jax.random.uniform(keys[1], (1, CELLS), jnp.float32, math.log(0.6), math.log(1.8)))
    base_level = jax.random.uniform(keys[2], (F, CELLS), jnp.float32, -3.0, 3.0)
    group_start_index = jax.random.uniform(keys[3], (GROUPS, F, CELLS), jnp.float32, -1.0, 1.0)
    noise = jnp.clip(jax.random.normal(keys[4], (DAYS, F, CELLS), jnp.float32), -4.0, 4.0)
    value = base_level[None] + ramp[:, None, None] * group_start_index[day_group] + feature_scale * cell_scale * noise
    return jnp.clip(value, -24.0, 24.0).astype(jnp.bfloat16)


def with_ends(array, stream_key, smallest, high):
    shape = array.shape
    spot = [jax.random.randint(jax.random.fold_in(stream_key, axis), (), 0, shape[axis]) for axis in range(len(shape))]
    array = array.at[tuple(spot)].set(smallest)
    longest = shape.index(max(shape))
    spot[longest] = (spot[longest] + 1) % shape[longest]
    return array.at[tuple(spot)].set(high)


def setup_inputs(seed: int = 0) -> dict:
    streams_of = jax.random.split(jax.random.key(seed), 4)
    readings = draw_readings(jax.random.fold_in(streams_of[3], 71), 0)
    cell_ids = jax.vmap(lambda own: jax.random.permutation(own, CELLS))(jax.random.split(streams_of[1], SLABS)).reshape((SLABS, CELLS)).astype(jnp.int32)
    valid_days = with_ends(jax.random.randint(streams_of[2], (SLABS,), 1, DS + 1), jax.random.fold_in(streams_of[2], 1), 1, DS).astype(jnp.int32)
    return dict(readings=readings, cell_ids=cell_ids, valid_days=valid_days)


def reference(readings, cell_ids, valid_days):
    cell_ordering = jnp.broadcast_to(jnp.arange(CELLS, dtype=jnp.int32)[None, :], (SLABS, CELLS))
    slab_rows = jnp.broadcast_to(jnp.arange(SLABS, dtype=jnp.int32)[:, None], (SLABS, CELLS))
    positions = jnp.zeros((SLABS, CELLS), jnp.int32).at[slab_rows, cell_ids].set(cell_ordering)
    slab_data = readings.reshape(SLABS, DS, F, CELLS)
    ordered = jax.vmap(lambda slab, where: jnp.take(slab, where, axis=2))(slab_data, positions)
    weights = (jnp.arange(DS, dtype=jnp.int32)[None, :] < valid_days[:, None]).astype(jnp.float32)
    repeats = SLABS // GROUPS
    weights = weights.reshape(repeats, GROUPS, DS)
    sample_counts = jnp.sum(weights, axis=(0, 2))
    total_count = jnp.sum(sample_counts)
    day_weight = weights[:, :, :, None, None]

    def per_block(block_index):
        piece = lax.dynamic_slice_in_dim(ordered, block_index * CPC, CPC, 3)
        block_values = piece.astype(jnp.float32).reshape(repeats, GROUPS, DS, F, CPC)
        group_sums = jnp.sum(day_weight * block_values, axis=(0, 2))
        group_mean = group_sums / sample_counts[:, None, None]
        anomaly = (block_values - group_mean[None, :, None]) * day_weight
        within = jnp.einsum('rgdfc,rgdhc->cfh', anomaly, anomaly, precision=lax.Precision.HIGHEST)
        total_mean = jnp.sum(group_sums, axis=0) / total_count
        start_index = group_mean - total_mean[None]
        between_groups = jnp.einsum('i,ixe,ike->exk', sample_counts, start_index, start_index, precision=lax.Precision.HIGHEST)
        return ((within + between_groups) / (total_count - 1.0)).reshape(CPC, F * F)

    result = lax.map(per_block, jnp.arange(N_CELL, dtype=jnp.int32))
    return result.reshape(CELLS, F * F)
```

```python
import functools

import jax
import jax.numpy as jnp
from jax import lax
from jax.experimental import pallas as pl
from jax.experimental.pallas import tpu as pltpu
from jax.sharding import PartitionSpec as P

LANES = 128
SKEW = 1
QUARTERS = 4
NT = (((1,), (1,)), ((), ()))


def kernel(
    cells_axis, tm_devices, readings_ref, ids_ref, valid_in_ref, out_ref,
    staged_ref, here_ref, valid_ref, ordered_ref, received_ref, anomaly_ref, square_ref,
    load_sem, local_sem, send_sem, recv_sem, late_sem, go_sem,
):
    devices = cells_axis * tm_devices
    span = tm_devices // QUARTERS
    plane = devices // QUARTERS
    my_cell = lax.axis_index("cell")
    my_tm = lax.axis_index("tm")
    me = my_cell * tm_devices + my_tm
    quarter = my_tm // span
    low = my_tm % span
    early = quarter < 2

    def place_of(to_quarter, step):
        to_cell = lax.rem(my_cell + step // span, cells_axis)
        to_tm = to_quarter * span + lax.rem(low + step % span, span)
        return to_cell * tm_devices + to_tm, {"cell": to_cell, "tm": to_tm}

    def signal_plane(sem, to_quarter, first=0):
        def one(step, carry):
            _, place = place_of(to_quarter, step)
            pl.semaphore_signal(sem, inc=1, device_id=place, device_id_type=pl.DeviceIdType.MESH)
            return carry

        lax.fori_loop(first, plane, one, 0, unroll=True if plane <= 8 else 1)

    load = pltpu.make_async_copy(readings_ref, staged_ref, load_sem.at[0])
    load.start()
    load_ids = pltpu.make_async_copy(ids_ref, here_ref, load_sem.at[1])
    load_ids.start()
    load_valid = pltpu.make_async_copy(valid_in_ref, valid_ref, load_sem.at[2])
    load_valid.start()
    barrier = pltpu.get_barrier_semaphore()

    @pl.when(early)
    def _():
        signal_plane(barrier, 2)
        signal_plane(barrier, 3)
        signal_plane(barrier, 1 - quarter)
        signal_plane(barrier, quarter, 1)

    @pl.when(quarter == 2)
    def _():
        signal_plane(barrier, 0)
        signal_plane(barrier, 1)

    load_ids.wait()
    load.wait()
    days, features, cells = readings_ref.shape
    owned = cells // devices
    main = features // LANES * LANES
    rest = features - main
    pieces = [staged_ref[d, :main, :] for d in range(days)]
    if rest:
        pieces += [staged_ref[d, main:, :] for d in range(days)]
    columns = jnp.concatenate(pieces, axis=0)
    ids = here_ref[...]
    block = min(cells, 256)
    for start in range(0, cells, block):
        cell = lax.broadcasted_iota(jnp.int32, (block, cells), 0) + start
        pick = jnp.where(cell == ids, 1.0, 0.0).astype(jnp.bfloat16)
        ordered = lax.dot_general(pick, columns, NT, preferred_element_type=jnp.float32)
        ordered_ref[start // owned : (start + block) // owned] = ordered.reshape(
            block // owned, owned, days * features
        ).astype(jnp.bfloat16)

    own = pltpu.make_async_copy(ordered_ref.at[me], received_ref.at[me], local_sem)
    own.start()

    def send(to_quarter, step):
        index, place = place_of(to_quarter, step)
        pltpu.make_async_remote_copy(
            src_ref=ordered_ref.at[index],
            dst_ref=received_ref.at[me],
            send_sem=send_sem,
            recv_sem=recv_sem,
            device_id=place,
            device_id_type=pl.DeviceIdType.MESH,
        ).start()

    def send_planes(parts):
        def one(step, carry):
            for to_quarter in parts:
                send(to_quarter, step)
            return carry

        lax.fori_loop(0, plane, one, 0)

    def send_own():
        def one(step, carry):
            send(quarter, step)
            return carry

        lax.fori_loop(1, plane, one, 0)

    partner = {"cell": my_cell, "tm": lax.rem(my_tm + tm_devices // 2, tm_devices)}

    @pl.when(early)
    def _():
        pl.semaphore_wait(barrier, 3 * plane - 1)
        send_own()
        send_planes([2, 1 - quarter])
        pl.semaphore_wait(late_sem, plane)
        pl.semaphore_signal(go_sem, inc=1, device_id=partner, device_id_type=pl.DeviceIdType.MESH)
        send_planes([3])

    @pl.when(jnp.logical_not(early))
    def _():
        pl.semaphore_wait(barrier, 2 * plane)

        @pl.when(quarter == 3)
        def _():
            signal_plane(late_sem, 1)
            signal_plane(late_sem, 0)

        send_planes([0])
        pl.semaphore_wait(go_sem, 1)
        send_own()
        send_planes([1, 5 - quarter])

    load_valid.wait()
    own.wait()
    others = pl.ds(0, devices - 1)
    pltpu.make_async_copy(received_ref.at[others], received_ref.at[others], recv_sem).wait()
    covariance(days, features, valid_ref, received_ref, out_ref, anomaly_ref, square_ref)
    pltpu.make_async_copy(ordered_ref.at[others], ordered_ref.at[others], send_sem).wait()


def covariance(days, features, valid_ref, received_ref, out_ref, anomaly_ref, square_ref):
    slabs, owned, width = received_ref.shape
    main = features // LANES * LANES
    rest = features - main
    tiles = width // LANES

    lane = lax.broadcasted_iota(jnp.int32, (owned, width), 1)
    day = lane // main if main else lane // rest
    if main and rest:
        day = jnp.where(lane < days * main, day, (lane - days * main) // rest)

    def add(slab, carry):
        total, count = carry
        valid = valid_ref[slab]
        value = received_ref[slab].astype(jnp.float32)
        return total + jnp.where(day < valid, value, 0.0), count + valid

    total, count = lax.fori_loop(
        0, slabs, add, (jnp.zeros((owned, width), jnp.float32), jnp.int32(0)), unroll=8
    )
    count = jnp.full((1, 1), count, jnp.int32).astype(jnp.float32)
    parts = []
    for start, size in ((0, main), (days * main, rest)):
        if size:
            part = total[:, start : start + size]
            for d in range(1, days):
                part = part + total[:, start + d * size : start + (d + 1) * size]
            parts += [part / count] * days
    mean = jnp.concatenate(parts, axis=1)

    def centre(slab, carry):
        value = received_ref[slab].astype(jnp.float32) - mean
        row = slab * (owned + SKEW)
        anomaly = jnp.where(day < valid_ref[slab], value, 0.0)
        for tile in range(tiles):
            piece = anomaly[:, tile * LANES : (tile + 1) * LANES]
            anomaly_ref[tile, pl.ds(row, owned), :] = piece
        return carry

    lax.fori_loop(0, slabs, centre, 0, unroll=8)

    scale = 1.0 / (count - 1.0)
    for cell in range(owned):
        rows = jnp.concatenate(
            [anomaly_ref[tile, pl.ds(cell, slabs, stride=owned + SKEW), :] for tile in range(tiles)],
            axis=1,
        )
        by_day = []
        for d in range(days):
            part = [rows[:, d * main : (d + 1) * main]] if main else []
            if rest:
                at = days * main + d * rest
                part.append(rows[:, at : at + rest])
            by_day.append(jnp.concatenate(part, axis=1))
        turned = jnp.concatenate(by_day, axis=0).T
        high = turned.astype(jnp.bfloat16)
        low = (turned - high.astype(jnp.float32)).astype(jnp.bfloat16)
        square = lax.dot_general(
            jnp.concatenate([high, high, low], axis=1),
            jnp.concatenate([high, low, high], axis=1),
            NT,
            preferred_element_type=jnp.float32,
        )
        square = square * scale
        for tile, start in enumerate(range(0, features, LANES)):
            size = min(LANES, features - start)
            square_ref[tile, cell * (features + SKEW) : cell * (features + SKEW) + features, :size] = square[
                :, start : start + size
            ]

    group = 4
    steps = features // group

    def lay_out(step, carry):
        first = step * group
        lines = []
        for i in range(group):
            for tile, start in enumerate(range(0, features, LANES)):
                line = square_ref[tile, pl.ds(first + i, owned, stride=features + SKEW), :]
                lines.append(line[:, : min(LANES, features - start)])
        at = pl.multiple_of(first * features, group * features)
        out_ref[:, pl.ds(at, group * features)] = jnp.concatenate(lines, axis=1)
        return carry

    lax.fori_loop(0, steps, lay_out, 0, unroll=True)


def on_device(readings, cell_ids, valid_days):
    tm_devices = lax.axis_size("tm")
    cells_axis = lax.axis_size("cell")
    devices = cells_axis * tm_devices
    days, features, cells = readings.shape
    owned = cells // devices
    width = days * features
    return pl.pallas_call(
        functools.partial(kernel, cells_axis, tm_devices),
        out_shape=pltpu.VMEM((owned, features * features), jnp.float32),
        in_specs=[pl.BlockSpec(memory_space=pltpu.HBM)] * 3,
        out_specs=pl.BlockSpec(memory_space=pltpu.VMEM),
        scratch_shapes=[
            pltpu.VMEM(readings.shape, jnp.bfloat16),
            pltpu.VMEM(cell_ids.shape, jnp.int32),
            pltpu.SMEM(valid_days.shape, jnp.int32),
            pltpu.VMEM((devices, owned, width), jnp.bfloat16),
            pltpu.VMEM((devices, owned, width), jnp.bfloat16),
            pltpu.VMEM((width // LANES, devices * (owned + SKEW), LANES), jnp.float32),
            pltpu.VMEM((pl.cdiv(features, LANES), owned * (features + SKEW), LANES), jnp.float32),
            pltpu.SemaphoreType.DMA((3,)),
            pltpu.SemaphoreType.DMA,
            pltpu.SemaphoreType.DMA,
            pltpu.SemaphoreType.DMA,
            pltpu.SemaphoreType.REGULAR,
            pltpu.SemaphoreType.REGULAR,
        ],
        compiler_params=pltpu.CompilerParams(
            collective_id=0, has_side_effects=True, vmem_limit_bytes=40 * 1024 * 1024
        ),
        name="covariance",
    )(*[pltpu.with_memory_space_constraint(a, pltpu.HBM) for a in (readings, cell_ids, valid_days)])


def solution(mesh):
    return jax.shard_map(
        on_device,
        mesh=mesh,
        in_specs=(P(("cell", "tm"), None, None), P(("cell", "tm"), None), P()),
        out_specs=P(("cell", "tm"), None),
        check_vma=False,
    )
```

```python
import functools

import jax
import jax.numpy as jnp
from jax import lax
from jax.experimental import pallas as pl
from jax.experimental.pallas import tpu as pltpu
from jax.sharding import PartitionSpec as P

LANES = 128
SKEW = 1
QUARTERS = 4
NT = (((1,), (1,)), ((), ()))


def kernel(
    cells_axis, tm_devices, readings_ref, ids_ref, valid_in_ref, out_ref,
    staged_ref, here_ref, valid_ref, ordered_ref, received_ref, anomaly_ref, square_ref,
    load_sem, local_sem, send_sem, recv_sem, late_sem, go_sem,
):
    devices = cells_axis * tm_devices
    span = tm_devices // QUARTERS
    plane = devices // QUARTERS
    my_cell = lax.axis_index("cell")
    my_tm = lax.axis_index("tm")
    me = my_cell * tm_devices + my_tm
    quarter = my_tm // span
    low = my_tm % span
    early = quarter < 2

    def place_of(to_quarter, step):
        to_cell = lax.rem(my_cell + step // span, cells_axis)
        to_tm = to_quarter * span + lax.rem(low + step % span, span)
        return to_cell * tm_devices + to_tm, {"cell": to_cell, "tm": to_tm}

    def signal_plane(sem, to_quarter, first=0):
        def one(step, carry):
            _, place = place_of(to_quarter, step)
            pl.semaphore_signal(sem, inc=1, device_id=place, device_id_type=pl.DeviceIdType.MESH)
            return carry

        lax.fori_loop(first, plane, one, 0, unroll=True if plane <= 8 else 1)

    load = pltpu.make_async_copy(readings_ref, staged_ref, load_sem.at[0])
    load.start()
    load_ids = pltpu.make_async_copy(ids_ref, here_ref, load_sem.at[1])
    load_ids.start()
    load_valid = pltpu.make_async_copy(valid_in_ref, valid_ref, load_sem.at[2])
    load_valid.start()
    barrier = pltpu.get_barrier_semaphore()

    @pl.when(early)
    def _():
        signal_plane(barrier, 2)
        signal_plane(barrier, 3)
        signal_plane(barrier, 1 - quarter)
        signal_plane(barrier, quarter, 1)

    @pl.when(jnp.logical_not(early))
    def _():
        signal_plane(barrier, 0)

    @pl.when(quarter == 2)
    def _():
        signal_plane(barrier, 1)

    load_ids.wait()
    load.wait()
    days, features, cells = readings_ref.shape
    owned = cells // devices
    main = features // LANES * LANES
    rest = features - main
    pieces = [staged_ref[d, :main, :] for d in range(days)]
    if rest:
        pieces += [staged_ref[d, main:, :] for d in range(days)]
    columns = jnp.concatenate(pieces, axis=0)
    ids = here_ref[...]
    block = min(cells, 256)
    for start in range(0, cells, block):
        cell = lax.broadcasted_iota(jnp.int32, (block, cells), 0) + start
        pick = jnp.where(cell == ids, 1.0, 0.0).astype(jnp.bfloat16)
        ordered = lax.dot_general(pick, columns, NT, preferred_element_type=jnp.float32)
        ordered_ref[start // owned : (start + block) // owned] = ordered.reshape(
            block // owned, owned, days * features
        ).astype(jnp.bfloat16)

    own = pltpu.make_async_copy(ordered_ref.at[me], received_ref.at[me], local_sem)
    own.start()

    def send(to_quarter, step):
        index, place = place_of(to_quarter, step)
        pltpu.make_async_remote_copy(
            src_ref=ordered_ref.at[index],
            dst_ref=received_ref.at[me],
            send_sem=send_sem,
            recv_sem=recv_sem,
            device_id=place,
            device_id_type=pl.DeviceIdType.MESH,
        ).start()

    def send_planes(parts):
        def one(step, carry):
            for to_quarter in parts:
                send(to_quarter, step)
            return carry

        lax.fori_loop(0, plane, one, 0)

    def send_own():
        def one(step, carry):
            send(quarter, step)
            return carry

        lax.fori_loop(1, plane, one, 0)

    def signal_go(to_quarter):
        place = {"cell": my_cell, "tm": to_quarter * span + low}
        pl.semaphore_signal(go_sem, inc=1, device_id=place, device_id_type=pl.DeviceIdType.MESH)

    @pl.when(quarter == 0)
    def _():
        pl.semaphore_wait(barrier, devices - 1)
        send_own()
        send_planes([2, 3])
        send_planes([1])

    @pl.when(quarter == 1)
    def _():
        pl.semaphore_wait(barrier, 3 * plane - 1)
        send_planes([2, 0])
        send_own()
        pl.semaphore_wait(late_sem, plane)
        signal_go(2)
        signal_go(3)
        send_planes([3])

    @pl.when(quarter == 2)
    def _():
        pl.semaphore_wait(barrier, 2 * plane)
        send_planes([0])
        send_planes([1])
        pl.semaphore_wait(go_sem, 1)
        send_planes([3])
        send_own()

    @pl.when(quarter == 3)
    def _():
        pl.semaphore_wait(barrier, 2 * plane)
        signal_plane(late_sem, 1)
        send_planes([0])
        pl.semaphore_wait(go_sem, 1)
        send_planes([1])
        send_planes([2])
        send_own()

    load_valid.wait()
    own.wait()
    others = pl.ds(0, devices - 1)
    pltpu.make_async_copy(received_ref.at[others], received_ref.at[others], recv_sem).wait()
    covariance(days, features, valid_ref, received_ref, out_ref, anomaly_ref, square_ref)
    pltpu.make_async_copy(ordered_ref.at[others], ordered_ref.at[others], send_sem).wait()


def covariance(days, features, valid_ref, received_ref, out_ref, anomaly_ref, square_ref):
    slabs, owned, width = received_ref.shape
    main = features // LANES * LANES
    rest = features - main
    tiles = width // LANES

    lane = lax.broadcasted_iota(jnp.int32, (owned, width), 1)
    day = lane // main if main else lane // rest
    if main and rest:
        day = jnp.where(lane < days * main, day, (lane - days * main) // rest)

    def add(slab, carry):
        total, count = carry
        valid = valid_ref[slab]
        value = received_ref[slab].astype(jnp.float32)
        return total + jnp.where(day < valid, value, 0.0), count + valid

    total, count = lax.fori_loop(
        0, slabs, add, (jnp.zeros((owned, width), jnp.float32), jnp.int32(0)), unroll=8
    )
    count = jnp.full((1, 1), count, jnp.int32).astype(jnp.float32)
    parts = []
    for start, size in ((0, main), (days * main, rest)):
        if size:
            part = total[:, start : start + size]
            for d in range(1, days):
                part = part + total[:, start + d * size : start + (d + 1) * size]
            parts += [part / count] * days
    mean = jnp.concatenate(parts, axis=1)

    def centre(slab, carry):
        value = received_ref[slab].astype(jnp.float32) - mean
        row = slab * (owned + SKEW)
        anomaly = jnp.where(day < valid_ref[slab], value, 0.0)
        for tile in range(tiles):
            piece = anomaly[:, tile * LANES : (tile + 1) * LANES]
            anomaly_ref[tile, pl.ds(row, owned), :] = piece
        return carry

    lax.fori_loop(0, slabs, centre, 0, unroll=8)

    scale = 1.0 / (count - 1.0)
    for cell in range(owned):
        rows = jnp.concatenate(
            [anomaly_ref[tile, pl.ds(cell, slabs, stride=owned + SKEW), :] for tile in range(tiles)],
            axis=1,
        )
        by_day = []
        for d in range(days):
            part = [rows[:, d * main : (d + 1) * main]] if main else []
            if rest:
                at = days * main + d * rest
                part.append(rows[:, at : at + rest])
            by_day.append(jnp.concatenate(part, axis=1))
        turned = jnp.concatenate(by_day, axis=0).T
        high = turned.astype(jnp.bfloat16)
        low = (turned - high.astype(jnp.float32)).astype(jnp.bfloat16)
        square = lax.dot_general(
            jnp.concatenate([high, high, low], axis=1),
            jnp.concatenate([high, low, high], axis=1),
            NT,
            preferred_element_type=jnp.float32,
        )
        square = square * scale
        for tile, start in enumerate(range(0, features, LANES)):
            size = min(LANES, features - start)
            square_ref[tile, cell * (features + SKEW) : cell * (features + SKEW) + features, :size] = square[
                :, start : start + size
            ]

    group = 4
    steps = features // group

    def lay_out(step, carry):
        first = step * group
        lines = []
        for i in range(group):
            for tile, start in enumerate(range(0, features, LANES)):
                line = square_ref[tile, pl.ds(first + i, owned, stride=features + SKEW), :]
                lines.append(line[:, : min(LANES, features - start)])
        at = pl.multiple_of(first * features, group * features)
        out_ref[:, pl.ds(at, group * features)] = jnp.concatenate(lines, axis=1)
        return carry

    lax.fori_loop(0, steps, lay_out, 0, unroll=True)


def on_device(readings, cell_ids, valid_days):
    tm_devices = lax.axis_size("tm")
    cells_axis = lax.axis_size("cell")
    devices = cells_axis * tm_devices
    days, features, cells = readings.shape
    owned = cells // devices
    width = days * features
    return pl.pallas_call(
        functools.partial(kernel, cells_axis, tm_devices),
        out_shape=pltpu.VMEM((owned, features * features), jnp.float32),
        in_specs=[pl.BlockSpec(memory_space=pltpu.HBM)] * 3,
        out_specs=pl.BlockSpec(memory_space=pltpu.VMEM),
        scratch_shapes=[
            pltpu.VMEM(readings.shape, jnp.bfloat16),
            pltpu.VMEM(cell_ids.shape, jnp.int32),
            pltpu.SMEM(valid_days.shape, jnp.int32),
            pltpu.VMEM((devices, owned, width), jnp.bfloat16),
            pltpu.VMEM((devices, owned, width), jnp.bfloat16),
            pltpu.VMEM((width // LANES, devices * (owned + SKEW), LANES), jnp.float32),
            pltpu.VMEM((pl.cdiv(features, LANES), owned * (features + SKEW), LANES), jnp.float32),
            pltpu.SemaphoreType.DMA((3,)),
            pltpu.SemaphoreType.DMA,
            pltpu.SemaphoreType.DMA,
            pltpu.SemaphoreType.DMA,
            pltpu.SemaphoreType.REGULAR,
            pltpu.SemaphoreType.REGULAR,
        ],
        compiler_params=pltpu.CompilerParams(
            collective_id=0, has_side_effects=True, vmem_limit_bytes=40 * 1024 * 1024
        ),
        name="covariance",
    )(*[pltpu.with_memory_space_constraint(a, pltpu.HBM) for a in (readings, cell_ids, valid_days)])


def solution(mesh):
    return jax.shard_map(
        on_device,
        mesh=mesh,
        in_specs=(P(("cell", "tm"), None, None), P(("cell", "tm"), None), P()),
        out_specs=P(("cell", "tm"), None),
        check_vma=False,
    )
```

```python
import functools

import jax
import jax.numpy as jnp
from jax import lax
from jax.experimental import pallas as pl
from jax.experimental.pallas import tpu as pltpu
from jax.sharding import PartitionSpec as P

LANES = 128
SKEW = 1
QUARTERS = 4
NT = (((1,), (1,)), ((), ()))


def kernel(
    cells_axis, tm_devices, readings_ref, ids_ref, valid_in_ref, anomaly_ref, weight_ref, mean_ref, scale_ref,
    staged_ref, here_ref, valid_ref, ordered_ref, received_ref,
    load_sem, local_sem, send_sem, recv_sem, late_sem, go_sem,
):
    devices = cells_axis * tm_devices
    span = tm_devices // QUARTERS
    plane = devices // QUARTERS
    my_cell = lax.axis_index("cell")
    my_tm = lax.axis_index("tm")
    me = my_cell * tm_devices + my_tm
    quarter = my_tm // span
    low = my_tm % span
    early = quarter < 2

    def place_of(to_quarter, step):
        to_cell = lax.rem(my_cell + step // span, cells_axis)
        to_tm = to_quarter * span + lax.rem(low + step % span, span)
        return to_cell * tm_devices + to_tm, {"cell": to_cell, "tm": to_tm}

    def signal_plane(sem, to_quarter, first=0):
        def one(step, carry):
            _, place = place_of(to_quarter, step)
            pl.semaphore_signal(sem, inc=1, device_id=place, device_id_type=pl.DeviceIdType.MESH)
            return carry

        lax.fori_loop(first, plane, one, 0, unroll=True if plane <= 8 else 1)

    load = pltpu.make_async_copy(readings_ref, staged_ref, load_sem.at[0])
    load.start()
    load_ids = pltpu.make_async_copy(ids_ref, here_ref, load_sem.at[1])
    load_ids.start()
    load_valid = pltpu.make_async_copy(valid_in_ref, valid_ref, load_sem.at[2])
    load_valid.start()
    barrier = pltpu.get_barrier_semaphore()

    @pl.when(early)
    def _():
        signal_plane(barrier, 2)
        signal_plane(barrier, 3)
        signal_plane(barrier, 1 - quarter)
        signal_plane(barrier, quarter, 1)

    @pl.when(jnp.logical_not(early))
    def _():
        signal_plane(barrier, 0)

    @pl.when(quarter == 2)
    def _():
        signal_plane(barrier, 1)

    load_ids.wait()
    load.wait()
    days, features, cells = readings_ref.shape
    owned = cells // devices
    main = features // LANES * LANES
    rest = features - main
    pieces = [staged_ref[d, :main, :] for d in range(days)]
    if rest:
        pieces += [staged_ref[d, main:, :] for d in range(days)]
    columns = jnp.concatenate(pieces, axis=0)
    ids = here_ref[...]
    block = min(cells, 256)
    for start in range(0, cells, block):
        cell = lax.broadcasted_iota(jnp.int32, (block, cells), 0) + start
        pick = jnp.where(cell == ids, 1.0, 0.0).astype(jnp.bfloat16)
        ordered = lax.dot_general(pick, columns, NT, preferred_element_type=jnp.float32)
        ordered_ref[start // owned : (start + block) // owned] = ordered.reshape(
            block // owned, owned, days * features
        ).astype(jnp.bfloat16)

    own = pltpu.make_async_copy(ordered_ref.at[me], received_ref.at[me], local_sem)
    own.start()

    def send(to_quarter, step):
        index, place = place_of(to_quarter, step)
        pltpu.make_async_remote_copy(
            src_ref=ordered_ref.at[index],
            dst_ref=received_ref.at[me],
            send_sem=send_sem,
            recv_sem=recv_sem.at[quarter],
            device_id=place,
            device_id_type=pl.DeviceIdType.MESH,
        ).start()

    def send_planes(parts):
        def one(step, carry):
            for to_quarter in parts:
                send(to_quarter, step)
            return carry

        lax.fori_loop(0, plane, one, 0)

    def send_own():
        def one(step, carry):
            send(quarter, step)
            return carry

        lax.fori_loop(1, plane, one, 0)

    def signal_go(to_quarter):
        place = {"cell": my_cell, "tm": to_quarter * span + low}
        pl.semaphore_signal(go_sem, inc=1, device_id=place, device_id_type=pl.DeviceIdType.MESH)

    @pl.when(quarter == 0)
    def _():
        pl.semaphore_wait(barrier, devices - 1)
        send_own()
        send_planes([2, 3])
        send_planes([1])

    @pl.when(quarter == 1)
    def _():
        pl.semaphore_wait(barrier, 3 * plane - 1)
        send_planes([2, 0])
        send_own()
        pl.semaphore_wait(late_sem, plane)
        signal_go(2)
        signal_go(3)
        send_planes([3])

    @pl.when(quarter == 2)
    def _():
        pl.semaphore_wait(barrier, 2 * plane)
        send_planes([0])
        send_planes([1])
        pl.semaphore_wait(go_sem, 1)
        send_planes([3])
        send_own()

    @pl.when(quarter == 3)
    def _():
        pl.semaphore_wait(barrier, 2 * plane)
        signal_plane(late_sem, 1)
        send_planes([0])
        pl.semaphore_wait(go_sem, 1)
        send_planes([1])
        send_planes([2])
        send_own()

    load_valid.wait()

    def arrive(source):
        @pl.when(source == quarter)
        def _():
            own.wait()
            less = pl.ds(0, plane - 1)
            pltpu.make_async_copy(
                received_ref.at[less], received_ref.at[less], recv_sem.at[source]
            ).wait()

        @pl.when(source != quarter)
        def _():
            every = pl.ds(0, plane)
            pltpu.make_async_copy(
                received_ref.at[every], received_ref.at[every], recv_sem.at[source]
            ).wait()

    order = range(QUARTERS)
    spread_all(
        days, features, span, arrive, order, valid_ref, received_ref, anomaly_ref, weight_ref, mean_ref,
        scale_ref,
    )
    others = pl.ds(0, devices - 1)
    pltpu.make_async_copy(ordered_ref.at[others], ordered_ref.at[others], send_sem).wait()


def spread_all(
    days, features, span, arrive, order, valid_ref, received_ref, anomaly_ref, weight_ref, mean_ref,
    scale_ref,
):
    slabs, owned, width = received_ref.shape
    main = features // LANES * LANES
    rest = features - main
    tiles = width // LANES

    lane = lax.broadcasted_iota(jnp.int32, (owned, width), 1)
    day = lane // main if main else lane // rest
    if main and rest:
        day = jnp.where(lane < days * main, day, (lane - days * main) // rest)

    def weigh(slab, count):
        valid = valid_ref[slab]
        weight = jnp.where(day[:1] < valid, 1.0, 0.0)
        for tile in range(tiles):
            weight_ref[tile, pl.ds(slab, 1), :] = weight[:, tile * LANES : (tile + 1) * LANES]
        return count + valid

    count = lax.fori_loop(0, slabs, weigh, jnp.int32(0), unroll=8)
    count = jnp.full((1, 1), count, jnp.int32).astype(jnp.float32)

    plane = slabs // QUARTERS
    apart = slabs // (plane // span)
    total = jnp.zeros((owned, width), jnp.float32)
    for source in order:
        arrive(source)

        for run in range(plane // span):
            first = run * apart + source * span

            def spread(slab, total):
                value = received_ref[slab].astype(jnp.float32)
                value = jnp.where(day < valid_ref[slab], value, 0.0)
                row = slab * (owned + SKEW)
                for tile in range(tiles):
                    piece = value[:, tile * LANES : (tile + 1) * LANES]
                    anomaly_ref[tile, pl.ds(row, owned), :] = piece
                return total + value

            total = lax.fori_loop(first, first + span, spread, total, unroll=True)

    parts = []
    for start, size in ((0, main), (days * main, rest)):
        if size:
            part = total[:, start : start + size]
            for d in range(1, days):
                part = part + total[:, start + d * size : start + (d + 1) * size]
            parts += [part / count] * days
    mean_ref[...] = jnp.concatenate(parts, axis=1)
    scale_ref[...] = jnp.broadcast_to(1.0 / (count - 1.0), scale_ref.shape)


def finish_kernel(
    days, features, anomaly_ref, weight_ref, mean_ref, scale_ref, out_ref,
    square_ref, laid_ref, out_sem,
):
    tiles, slabs, _ = weight_ref.shape
    owned = out_ref.shape[0]
    main = features // LANES * LANES
    rest = features - main
    scale = scale_ref[:1, :1]

    def turn(cell):
        rows = jnp.concatenate(
            [
                anomaly_ref[tile, pl.ds(cell, slabs, stride=owned + SKEW), :]
                - weight_ref[tile] * mean_ref[cell : cell + 1, tile * LANES : (tile + 1) * LANES]
                for tile in range(tiles)
            ],
            axis=1,
        )
        by_day = []
        for d in range(days):
            part = [rows[:, d * main : (d + 1) * main]] if main else []
            if rest:
                at = days * main + d * rest
                part.append(rows[:, at : at + rest])
            by_day.append(jnp.concatenate(part, axis=1))
        natural = jnp.concatenate(by_day, axis=0)
        flat = natural.astype(jnp.bfloat16)
        less = (natural - flat.astype(jnp.float32)).astype(jnp.bfloat16)
        turned = natural.T
        high = turned.astype(jnp.bfloat16)
        low = (turned - high.astype(jnp.float32)).astype(jnp.bfloat16)
        return high, low, flat, less

    def multiply(cell, high, low, flat, less):
        square = jnp.dot(
            jnp.concatenate([high, high, low], axis=1),
            jnp.concatenate([flat, less, flat], axis=0),
            preferred_element_type=jnp.float32,
        )
        square = square * scale
        at = cell * (features + SKEW)
        for tile, start in enumerate(range(0, features, LANES)):
            size = min(LANES, features - start)
            square_ref[tile, at : at + features, :size] = square[:, start : start + size]

    group = 4
    chunks = out_sem.shape[0]
    steps = features // group // chunks

    def lay_out(step, carry):
        first = step * group
        lines = []
        for i in range(group):
            for tile, start in enumerate(range(0, features, LANES)):
                line = square_ref[tile, pl.ds(first + i, owned, stride=features + SKEW), :]
                lines.append(line[:, : min(LANES, features - start)])
        at = pl.multiple_of(first * features, group * features)
        laid_ref[:, pl.ds(at, group * features)] = jnp.concatenate(lines, axis=1)
        return carry

    copies = []

    def give(chunk):
        lax.fori_loop(chunk * steps, (chunk + 1) * steps, lay_out, 0, unroll=True)
        size = steps * group * features
        at = pl.ds(chunk * size, size)
        copies.append(
            pltpu.make_async_copy(laid_ref.at[:, at], out_ref.at[:, at], out_sem.at[chunk])
        )
        copies[-1].start()

    for cell in range(owned):
        multiply(cell, *turn(cell))
    for chunk in range(chunks):
        give(chunk)
    for copy in copies:
        copy.wait()


def on_device(readings, cell_ids, valid_days):
    tm_devices = lax.axis_size("tm")
    cells_axis = lax.axis_size("cell")
    devices = cells_axis * tm_devices
    days, features, cells = readings.shape
    owned = cells // devices
    width = days * features
    tiles = width // LANES
    parts = pl.pallas_call(
        functools.partial(kernel, cells_axis, tm_devices),
        out_shape=(
            pltpu.VMEM((tiles, devices * (owned + SKEW), LANES), jnp.float32),
            pltpu.VMEM((tiles, devices, LANES), jnp.float32),
            pltpu.VMEM((owned, width), jnp.float32),
            pltpu.VMEM((owned, LANES), jnp.float32),
        ),
        in_specs=[pl.BlockSpec(memory_space=pltpu.HBM)] * 3,
        out_specs=[pl.BlockSpec(memory_space=pltpu.VMEM)] * 4,
        scratch_shapes=[
            pltpu.VMEM(readings.shape, jnp.bfloat16),
            pltpu.VMEM(cell_ids.shape, jnp.int32),
            pltpu.SMEM(valid_days.shape, jnp.int32),
            pltpu.VMEM((devices, owned, width), jnp.bfloat16),
            pltpu.VMEM((devices, owned, width), jnp.bfloat16),
            pltpu.SemaphoreType.DMA((3,)),
            pltpu.SemaphoreType.DMA,
            pltpu.SemaphoreType.DMA,
            pltpu.SemaphoreType.DMA((QUARTERS,)),
            pltpu.SemaphoreType.REGULAR,
            pltpu.SemaphoreType.REGULAR,
        ],
        compiler_params=pltpu.CompilerParams(
            collective_id=0, has_side_effects=True, vmem_limit_bytes=40 * 1024 * 1024
        ),
        name="exchange",
    )(*[pltpu.with_memory_space_constraint(a, pltpu.HBM) for a in (readings, cell_ids, valid_days)])

    return pl.pallas_call(
        functools.partial(finish_kernel, days, features),
        out_shape=jax.ShapeDtypeStruct((owned, features * features), jnp.float32),
        in_specs=[pl.BlockSpec(memory_space=pltpu.VMEM)] * 4,
        out_specs=pl.BlockSpec(memory_space=pl.ANY),
        scratch_shapes=[
            pltpu.VMEM((pl.cdiv(features, LANES), owned * (features + SKEW), LANES), jnp.float32),
            pltpu.VMEM((owned, features * features), jnp.float32),
            pltpu.SemaphoreType.DMA((5,)),
        ],
        compiler_params=pltpu.CompilerParams(vmem_limit_bytes=24 * 1024 * 1024),
        name="finish",
    )(*[pltpu.with_memory_space_constraint(part, pltpu.VMEM) for part in parts])


def solution(mesh):
    return jax.shard_map(
        on_device,
        mesh=mesh,
        in_specs=(P(("cell", "tm"), None, None), P(("cell", "tm"), None), P()),
        out_specs=P(("cell", "tm"), None),
        check_vma=False,
    )
```

```python
import functools

import jax
import jax.numpy as jnp
from jax import lax
from jax.experimental import pallas as pl
from jax.experimental.pallas import tpu as pltpu
from jax.sharding import PartitionSpec as P

LANES = 128
SKEW = 1
QUARTERS = 4
NT = (((1,), (1,)), ((), ()))


def kernel(
    cells_axis, tm_devices, readings_ref, ids_ref, valid_in_ref, anomaly_ref, weight_ref, mean_ref, scale_ref,
    staged_ref, here_ref, valid_ref, ordered_ref, received_ref,
    load_sem, local_sem, send_sem, recv_sem, late_sem, go_sem,
):
    devices = cells_axis * tm_devices
    span = tm_devices // QUARTERS
    plane = devices // QUARTERS
    my_cell = lax.axis_index("cell")
    my_tm = lax.axis_index("tm")
    me = my_cell * tm_devices + my_tm
    quarter = my_tm // span
    low = my_tm % span
    early = quarter < 2

    def place_of(to_quarter, step):
        to_cell = lax.rem(my_cell + step // span, cells_axis)
        to_tm = to_quarter * span + lax.rem(low + step % span, span)
        return to_cell * tm_devices + to_tm, {"cell": to_cell, "tm": to_tm}

    def signal_plane(sem, to_quarter, first=0):
        def one(step, carry):
            _, place = place_of(to_quarter, step)
            pl.semaphore_signal(sem, inc=1, device_id=place, device_id_type=pl.DeviceIdType.MESH)
            return carry

        lax.fori_loop(first, plane, one, 0, unroll=True if plane <= 8 else 1)

    load = pltpu.make_async_copy(readings_ref, staged_ref, load_sem.at[0])
    load.start()
    load_ids = pltpu.make_async_copy(ids_ref, here_ref, load_sem.at[1])
    load_ids.start()
    load_valid = pltpu.make_async_copy(valid_in_ref, valid_ref, load_sem.at[2])
    load_valid.start()
    barrier = pltpu.get_barrier_semaphore()

    @pl.when(early)
    def _():
        signal_plane(barrier, 2)
        signal_plane(barrier, 3)
        signal_plane(barrier, 1 - quarter)
        signal_plane(barrier, quarter, 1)

    @pl.when(jnp.logical_not(early))
    def _():
        signal_plane(barrier, 0)

    @pl.when(quarter == 2)
    def _():
        signal_plane(barrier, 1)

    load_ids.wait()
    load.wait()
    days, features, cells = readings_ref.shape
    owned = cells // devices
    main = features // LANES * LANES
    rest = features - main
    pieces = [staged_ref[d, :main, :] for d in range(days)]
    if rest:
        pieces += [staged_ref[d, main:, :] for d in range(days)]
    columns = jnp.concatenate(pieces, axis=0)
    ids = here_ref[...]
    block = min(cells, 256)
    for start in range(0, cells, block):
        cell = lax.broadcasted_iota(jnp.int32, (block, cells), 0) + start
        pick = jnp.where(cell == ids, 1.0, 0.0).astype(jnp.bfloat16)
        ordered = lax.dot_general(pick, columns, NT, preferred_element_type=jnp.float32)
        ordered_ref[start // owned : (start + block) // owned] = ordered.reshape(
            block // owned, owned, days * features
        ).astype(jnp.bfloat16)

    own = pltpu.make_async_copy(ordered_ref.at[me], received_ref.at[me], local_sem)
    own.start()

    def send(to_quarter, step):
        index, place = place_of(to_quarter, step)
        pltpu.make_async_remote_copy(
            src_ref=ordered_ref.at[index],
            dst_ref=received_ref.at[me],
            send_sem=send_sem,
            recv_sem=recv_sem.at[quarter],
            device_id=place,
            device_id_type=pl.DeviceIdType.MESH,
        ).start()

    def send_planes(parts, first=0, last=plane):
        def one(step, carry):
            for to_quarter in parts:
                send(to_quarter, step)
            return carry

        lax.fori_loop(first, last, one, 0)

    def send_own():
        def one(step, carry):
            send(quarter, step)
            return carry

        lax.fori_loop(1, plane, one, 0)

    def signal_go(to_quarter):
        place = {"cell": my_cell, "tm": to_quarter * span + low}
        pl.semaphore_signal(go_sem, inc=1, device_id=place, device_id_type=pl.DeviceIdType.MESH)

    @pl.when(quarter == 0)
    def _():
        pl.semaphore_wait(barrier, devices - 1)
        send_planes([3])
        send_own()
        send_planes([2])
        send_planes([1])

    @pl.when(quarter == 1)
    def _():
        pl.semaphore_wait(barrier, 3 * plane - 1)
        send_planes([2, 0])
        send_own()
        pl.semaphore_wait(late_sem, plane)
        signal_go(2)
        signal_go(3)
        send_planes([3])

    @pl.when(quarter == 2)
    def _():
        pl.semaphore_wait(barrier, 2 * plane)
        send_planes([0])
        send_planes([1])
        pl.semaphore_wait(go_sem, 1)
        send_planes([3])
        send_own()

    @pl.when(quarter == 3)
    def _():
        pl.semaphore_wait(barrier, 2 * plane)
        signal_plane(late_sem, 1)
        send_planes([0])
        send_planes([1], plane * 0 // 8, plane * 3 // 8)
        pl.semaphore_wait(go_sem, 1)
        send_planes([1], plane * 3 // 8, plane * 8 // 8)
        send_planes([2])
        send_own()

    load_valid.wait()

    def arrive(source):
        @pl.when(source == quarter)
        def _():
            own.wait()
            less = pl.ds(0, plane - 1)
            pltpu.make_async_copy(
                received_ref.at[less], received_ref.at[less], recv_sem.at[source]
            ).wait()

        @pl.when(source != quarter)
        def _():
            every = pl.ds(0, plane)
            pltpu.make_async_copy(
                received_ref.at[every], received_ref.at[every], recv_sem.at[source]
            ).wait()

    order = range(QUARTERS)
    spread_all(
        days, features, span, arrive, order, valid_ref, received_ref, anomaly_ref, weight_ref, mean_ref,
        scale_ref,
    )
    others = pl.ds(0, devices - 1)
    pltpu.make_async_copy(ordered_ref.at[others], ordered_ref.at[others], send_sem).wait()


def spread_all(
    days, features, span, arrive, order, valid_ref, received_ref, anomaly_ref, weight_ref, mean_ref,
    scale_ref,
):
    slabs, owned, width = received_ref.shape
    main = features // LANES * LANES
    rest = features - main
    tiles = width // LANES

    lane = lax.broadcasted_iota(jnp.int32, (owned, width), 1)
    day = lane // main if main else lane // rest
    if main and rest:
        day = jnp.where(lane < days * main, day, (lane - days * main) // rest)

    def weigh(slab, count):
        valid = valid_ref[slab]
        weight = jnp.where(day[:1] < valid, 1.0, 0.0)
        for tile in range(tiles):
            weight_ref[tile, pl.ds(slab, 1), :] = weight[:, tile * LANES : (tile + 1) * LANES]
        return count + valid

    count = lax.fori_loop(0, slabs, weigh, jnp.int32(0), unroll=8)
    count = jnp.full((1, 1), count, jnp.int32).astype(jnp.float32)

    plane = slabs // QUARTERS
    apart = slabs // (plane // span)
    total = jnp.zeros((owned, width), jnp.float32)
    for source in order:
        arrive(source)

        for run in range(plane // span):
            first = run * apart + source * span

            def spread(slab, total):
                value = received_ref[slab].astype(jnp.float32)
                value = jnp.where(day < valid_ref[slab], value, 0.0)
                row = slab * (owned + SKEW)
                for tile in range(tiles):
                    piece = value[:, tile * LANES : (tile + 1) * LANES]
                    anomaly_ref[tile, pl.ds(row, owned), :] = piece
                return total + value

            total = lax.fori_loop(first, first + span, spread, total, unroll=True)

    parts = []
    for start, size in ((0, main), (days * main, rest)):
        if size:
            part = total[:, start : start + size]
            for d in range(1, days):
                part = part + total[:, start + d * size : start + (d + 1) * size]
            parts += [part / count] * days
    mean_ref[...] = jnp.concatenate(parts, axis=1)
    scale_ref[...] = jnp.broadcast_to(1.0 / (count - 1.0), scale_ref.shape)


def finish_kernel(
    days, features, anomaly_ref, weight_ref, mean_ref, scale_ref, out_ref,
    square_ref, laid_ref, out_sem,
):
    tiles, slabs, _ = weight_ref.shape
    owned = out_ref.shape[0]
    main = features // LANES * LANES
    rest = features - main
    scale = scale_ref[:1, :1]

    def turn(cell):
        rows = jnp.concatenate(
            [
                anomaly_ref[tile, pl.ds(cell, slabs, stride=owned + SKEW), :]
                - weight_ref[tile] * mean_ref[cell : cell + 1, tile * LANES : (tile + 1) * LANES]
                for tile in range(tiles)
            ],
            axis=1,
        )
        by_day = []
        for d in range(days):
            part = [rows[:, d * main : (d + 1) * main]] if main else []
            if rest:
                at = days * main + d * rest
                part.append(rows[:, at : at + rest])
            by_day.append(jnp.concatenate(part, axis=1))
        natural = jnp.concatenate(by_day, axis=0)
        flat = natural.astype(jnp.bfloat16)
        less = (natural - flat.astype(jnp.float32)).astype(jnp.bfloat16)
        turned = natural.T
        high = turned.astype(jnp.bfloat16)
        low = (turned - high.astype(jnp.float32)).astype(jnp.bfloat16)
        return high, low, flat, less

    def multiply(cell, high, low, flat, less):
        square = jnp.dot(
            jnp.concatenate([high, high, low], axis=1),
            jnp.concatenate([flat, less, flat], axis=0),
            preferred_element_type=jnp.float32,
        )
        square = square * scale
        at = cell * (features + SKEW)
        for tile, start in enumerate(range(0, features, LANES)):
            size = min(LANES, features - start)
            square_ref[tile, at : at + features, :size] = square[:, start : start + size]

    group = 4
    chunks = out_sem.shape[0]
    steps = features // group // chunks

    def lay_out(step, carry):
        first = step * group
        lines = []
        for i in range(group):
            for tile, start in enumerate(range(0, features, LANES)):
                line = square_ref[tile, pl.ds(first + i, owned, stride=features + SKEW), :]
                lines.append(line[:, : min(LANES, features - start)])
        at = pl.multiple_of(first * features, group * features)
        laid_ref[:, pl.ds(at, group * features)] = jnp.concatenate(lines, axis=1)
        return carry

    copies = []

    def give(chunk):
        lax.fori_loop(chunk * steps, (chunk + 1) * steps, lay_out, 0, unroll=True)
        size = steps * group * features
        at = pl.ds(chunk * size, size)
        copies.append(
            pltpu.make_async_copy(laid_ref.at[:, at], out_ref.at[:, at], out_sem.at[chunk])
        )
        copies[-1].start()

    for cell in range(owned):
        multiply(cell, *turn(cell))
    for chunk in range(chunks):
        give(chunk)
    for copy in copies:
        copy.wait()


def on_device(readings, cell_ids, valid_days):
    tm_devices = lax.axis_size("tm")
    cells_axis = lax.axis_size("cell")
    devices = cells_axis * tm_devices
    days, features, cells = readings.shape
    owned = cells // devices
    width = days * features
    tiles = width // LANES
    parts = pl.pallas_call(
        functools.partial(kernel, cells_axis, tm_devices),
        out_shape=(
            pltpu.VMEM((tiles, devices * (owned + SKEW), LANES), jnp.float32),
            pltpu.VMEM((tiles, devices, LANES), jnp.float32),
            pltpu.VMEM((owned, width), jnp.float32),
            pltpu.VMEM((owned, LANES), jnp.float32),
        ),
        in_specs=[pl.BlockSpec(memory_space=pltpu.HBM)] * 3,
        out_specs=[pl.BlockSpec(memory_space=pltpu.VMEM)] * 4,
        scratch_shapes=[
            pltpu.VMEM(readings.shape, jnp.bfloat16),
            pltpu.VMEM(cell_ids.shape, jnp.int32),
            pltpu.SMEM(valid_days.shape, jnp.int32),
            pltpu.VMEM((devices, owned, width), jnp.bfloat16),
            pltpu.VMEM((devices, owned, width), jnp.bfloat16),
            pltpu.SemaphoreType.DMA((3,)),
            pltpu.SemaphoreType.DMA,
            pltpu.SemaphoreType.DMA,
            pltpu.SemaphoreType.DMA((QUARTERS,)),
            pltpu.SemaphoreType.REGULAR,
            pltpu.SemaphoreType.REGULAR,
        ],
        compiler_params=pltpu.CompilerParams(
            collective_id=0, has_side_effects=True, vmem_limit_bytes=40 * 1024 * 1024
        ),
        name="exchange",
    )(*[pltpu.with_memory_space_constraint(a, pltpu.HBM) for a in (readings, cell_ids, valid_days)])

    return pl.pallas_call(
        functools.partial(finish_kernel, days, features),
        out_shape=jax.ShapeDtypeStruct((owned, features * features), jnp.float32),
        in_specs=[pl.BlockSpec(memory_space=pltpu.VMEM)] * 4,
        out_specs=pl.BlockSpec(memory_space=pl.ANY),
        scratch_shapes=[
            pltpu.VMEM((pl.cdiv(features, LANES), owned * (features + SKEW), LANES), jnp.float32),
            pltpu.VMEM((owned, features * features), jnp.float32),
            pltpu.SemaphoreType.DMA((5,)),
        ],
        compiler_params=pltpu.CompilerParams(vmem_limit_bytes=24 * 1024 * 1024),
        name="finish",
    )(*[pltpu.with_memory_space_constraint(part, pltpu.VMEM) for part in parts])


def solution(mesh):
    return jax.shard_map(
        on_device,
        mesh=mesh,
        in_specs=(P(("cell", "tm"), None, None), P(("cell", "tm"), None), P()),
        out_specs=P(("cell", "tm"), None),
        check_vma=False,
    )
```

```python
import functools

import jax
import jax.numpy as jnp
from jax import lax
from jax.experimental import pallas as pl
from jax.experimental.pallas import tpu as pltpu
from jax.sharding import PartitionSpec as P

LANES = 128
SKEW = 1
QUARTERS = 4
NT = (((1,), (1,)), ((), ()))


def kernel(
    cells_axis, tm_devices, readings_ref, ids_ref, valid_in_ref, anomaly_ref, weight_ref, mean_ref, scale_ref,
    staged_ref, here_ref, valid_ref, ordered_ref, received_ref,
    load_sem, local_sem, send_sem, recv_sem, late_sem, go_sem,
):
    devices = cells_axis * tm_devices
    span = tm_devices // QUARTERS
    plane = devices // QUARTERS
    my_cell = lax.axis_index("cell")
    my_tm = lax.axis_index("tm")
    me = my_cell * tm_devices + my_tm
    quarter = my_tm // span
    low = my_tm % span
    early = quarter < 2

    def place_of(to_quarter, step):
        to_cell = lax.rem(my_cell + step // span, cells_axis)
        to_tm = to_quarter * span + lax.rem(low + step % span, span)
        return to_cell * tm_devices + to_tm, {"cell": to_cell, "tm": to_tm}

    def signal_plane(sem, to_quarter, first=0):
        def one(step, carry):
            _, place = place_of(to_quarter, step)
            pl.semaphore_signal(sem, inc=1, device_id=place, device_id_type=pl.DeviceIdType.MESH)
            return carry

        lax.fori_loop(first, plane, one, 0, unroll=True if plane <= 8 else 1)

    load = pltpu.make_async_copy(readings_ref, staged_ref, load_sem.at[0])
    load.start()
    load_ids = pltpu.make_async_copy(ids_ref, here_ref, load_sem.at[1])
    load_ids.start()
    load_valid = pltpu.make_async_copy(valid_in_ref, valid_ref, load_sem.at[2])
    load_valid.start()
    barrier = pltpu.get_barrier_semaphore()

    @pl.when(early)
    def _():
        signal_plane(barrier, 2)
        signal_plane(barrier, 3)
        signal_plane(barrier, 1 - quarter)
        signal_plane(barrier, quarter, 1)

    @pl.when(jnp.logical_not(early))
    def _():
        signal_plane(barrier, 0)

    @pl.when(quarter == 2)
    def _():
        signal_plane(barrier, 1)

    load_ids.wait()
    load.wait()
    days, features, cells = readings_ref.shape
    owned = cells // devices
    main = features // LANES * LANES
    rest = features - main
    pieces = [staged_ref[d, :main, :] for d in range(days)]
    if rest:
        pieces += [staged_ref[d, main:, :] for d in range(days)]
    columns = jnp.concatenate(pieces, axis=0)
    ids = here_ref[...]
    block = min(cells, 256)
    for start in range(0, cells, block):
        cell = lax.broadcasted_iota(jnp.int32, (block, cells), 0) + start
        pick = jnp.where(cell == ids, 1.0, 0.0).astype(jnp.bfloat16)
        ordered = lax.dot_general(pick, columns, NT, preferred_element_type=jnp.float32)
        ordered_ref[start // owned : (start + block) // owned] = ordered.reshape(
            block // owned, owned, days * features
        ).astype(jnp.bfloat16)

    own = pltpu.make_async_copy(ordered_ref.at[me], received_ref.at[me], local_sem)
    own.start()

    def send(to_quarter, step):
        index, place = place_of(to_quarter, step)
        pltpu.make_async_remote_copy(
            src_ref=ordered_ref.at[index],
            dst_ref=received_ref.at[me],
            send_sem=send_sem,
            recv_sem=recv_sem.at[quarter],
            device_id=place,
            device_id_type=pl.DeviceIdType.MESH,
        ).start()

    def send_planes(parts, first=0, last=plane):
        def one(step, carry):
            for to_quarter in parts:
                send(to_quarter, step)
            return carry

        lax.fori_loop(first, last, one, 0)

    def send_own():
        def one(step, carry):
            send(quarter, step)
            return carry

        lax.fori_loop(1, plane, one, 0)

    def signal_go(to_quarter):
        place = {"cell": my_cell, "tm": to_quarter * span + low}
        pl.semaphore_signal(go_sem, inc=1, device_id=place, device_id_type=pl.DeviceIdType.MESH)

    @pl.when(quarter == 0)
    def _():
        pl.semaphore_wait(barrier, devices - 1)
        send_planes([3])
        send_own()
        send_planes([2])
        send_planes([1])

    @pl.when(quarter == 1)
    def _():
        pl.semaphore_wait(barrier, 3 * plane - 1)
        send_planes([2, 0])
        send_own()
        pl.semaphore_wait(late_sem, plane)
        signal_go(2)
        signal_go(3)
        send_planes([3])

    @pl.when(quarter == 2)
    def _():
        pl.semaphore_wait(barrier, 2 * plane)
        send_planes([0])
        send_planes([1])
        pl.semaphore_wait(go_sem, 1)
        send_planes([3])
        send_own()

    @pl.when(quarter == 3)
    def _():
        pl.semaphore_wait(barrier, 2 * plane)
        signal_plane(late_sem, 1)
        send_planes([0])
        send_planes([1], plane * 0 // 8, plane * 3 // 8)
        pl.semaphore_wait(go_sem, 1)
        send_planes([1], plane * 3 // 8, plane * 8 // 8)
        send_planes([2])
        send_own()

    load_valid.wait()

    def arrive(source):
        @pl.when(source == quarter)
        def _():
            own.wait()
            less = pl.ds(0, plane - 1)
            pltpu.make_async_copy(
                received_ref.at[less], received_ref.at[less], recv_sem.at[source]
            ).wait()

        @pl.when(source != quarter)
        def _():
            every = pl.ds(0, plane)
            pltpu.make_async_copy(
                received_ref.at[every], received_ref.at[every], recv_sem.at[source]
            ).wait()

    order = range(QUARTERS)
    spread_all(
        days, features, span, arrive, order, valid_ref, received_ref, anomaly_ref, weight_ref, mean_ref,
        scale_ref,
    )
    others = pl.ds(0, devices - 1)
    pltpu.make_async_copy(ordered_ref.at[others], ordered_ref.at[others], send_sem).wait()


def spread_all(
    days, features, span, arrive, order, valid_ref, received_ref, anomaly_ref, weight_ref, mean_ref,
    scale_ref,
):
    slabs, owned, width = received_ref.shape
    main = features // LANES * LANES
    rest = features - main

    lane = lax.broadcasted_iota(jnp.int32, (owned, width), 1)
    day = lane // main if main else lane // rest
    if main and rest:
        day = jnp.where(lane < days * main, day, (lane - days * main) // rest)

    def weigh(slab, count):
        valid = valid_ref[slab]
        for d in range(days):
            weight_ref[d, pl.ds(slab, 1), :] = jnp.full((1, LANES), d < valid).astype(jnp.float32)
        return count + valid

    count = lax.fori_loop(0, slabs, weigh, jnp.int32(0), unroll=8)
    count = jnp.full((1, 1), count, jnp.int32).astype(jnp.float32)

    plane = slabs // QUARTERS
    apart = slabs // (plane // span)
    total = jnp.zeros((owned, width), jnp.float32)
    for source in order:
        arrive(source)

        for run in range(plane // span):
            first = run * apart + source * span

            def spread(slab, total):
                value = received_ref[slab].astype(jnp.float32)
                value = jnp.where(day < valid_ref[slab], value, 0.0)
                row = slab * (owned + SKEW)
                for tile in range(days * main // LANES):
                    piece = value[:, tile * LANES : (tile + 1) * LANES]
                    anomaly_ref[tile, pl.ds(row, owned), :] = piece
                if rest:
                    for d in range(days):
                        at = days * main + d * rest
                        tile = days * main // LANES + d
                        anomaly_ref[tile, pl.ds(row, owned), :rest] = value[:, at : at + rest]
                return total + value

            total = lax.fori_loop(first, first + span, spread, total, unroll=True)

    parts = []
    for start, size in ((0, main), (days * main, rest)):
        if size:
            part = total[:, start : start + size]
            for d in range(1, days):
                part = part + total[:, start + d * size : start + (d + 1) * size]
            parts.append(part / count)
    mean_ref[...] = jnp.concatenate(parts, axis=1)
    scale_ref[...] = jnp.broadcast_to(1.0 / (count - 1.0), scale_ref.shape)


def finish_kernel(
    days, features, anomaly_ref, weight_ref, mean_ref, scale_ref, out_ref,
    square_ref, laid_ref, out_sem,
):
    _, slabs, _ = weight_ref.shape
    owned = out_ref.shape[0]
    main = features // LANES * LANES
    scale = scale_ref[:1, :1]

    def turn(cell):
        by_day = []
        for d in range(days):
            part = []
            for tile in range(pl.cdiv(features, LANES)):
                at = tile * LANES
                size = min(LANES, features - at)
                index = d * (main // LANES) + tile if size == LANES else days * main // LANES + d
                rows = anomaly_ref[index, pl.ds(cell, slabs, stride=owned + SKEW), :]
                part.append(rows[:, :size] - weight_ref[d, :, :size] * mean_ref[cell : cell + 1, at : at + size])
            by_day.append(jnp.concatenate(part, axis=1))
        natural = jnp.concatenate(by_day, axis=0)
        flat = natural.astype(jnp.bfloat16)
        less = (natural - flat.astype(jnp.float32)).astype(jnp.bfloat16)
        turned = natural.T
        high = turned.astype(jnp.bfloat16)
        low = (turned - high.astype(jnp.float32)).astype(jnp.bfloat16)
        return high, low, flat, less

    def multiply(cell, high, low, flat, less):
        square = jnp.dot(
            jnp.concatenate([high, high, low], axis=1),
            jnp.concatenate([flat, less, flat], axis=0),
            preferred_element_type=jnp.float32,
        )
        square = square * scale
        at = cell * (features + SKEW)
        for tile, start in enumerate(range(0, features, LANES)):
            size = min(LANES, features - start)
            square_ref[tile, at : at + features, :size] = square[:, start : start + size]

    group = 4
    chunks = out_sem.shape[0]
    steps = features // group // chunks

    def lay_out(step, carry):
        first = step * group
        lines = []
        for i in range(group):
            for tile, start in enumerate(range(0, features, LANES)):
                line = square_ref[tile, pl.ds(first + i, owned, stride=features + SKEW), :]
                lines.append(line[:, : min(LANES, features - start)])
        at = pl.multiple_of(first * features, group * features)
        laid_ref[:, pl.ds(at, group * features)] = jnp.concatenate(lines, axis=1)
        return carry

    copies = []

    def give(chunk):
        lax.fori_loop(chunk * steps, (chunk + 1) * steps, lay_out, 0, unroll=True)
        size = steps * group * features
        at = pl.ds(chunk * size, size)
        copies.append(
            pltpu.make_async_copy(laid_ref.at[:, at], out_ref.at[:, at], out_sem.at[chunk])
        )
        copies[-1].start()

    for cell in range(owned):
        multiply(cell, *turn(cell))
    for chunk in range(chunks):
        give(chunk)
    for copy in copies:
        copy.wait()


def on_device(readings, cell_ids, valid_days):
    tm_devices = lax.axis_size("tm")
    cells_axis = lax.axis_size("cell")
    devices = cells_axis * tm_devices
    days, features, cells = readings.shape
    owned = cells // devices
    width = days * features
    tiles = days * pl.cdiv(features, LANES)
    parts = pl.pallas_call(
        functools.partial(kernel, cells_axis, tm_devices),
        out_shape=(
            pltpu.VMEM((tiles, devices * (owned + SKEW), LANES), jnp.float32),
            pltpu.VMEM((days, devices, LANES), jnp.float32),
            pltpu.VMEM((owned, features), jnp.float32),
            pltpu.VMEM((owned, LANES), jnp.float32),
        ),
        in_specs=[pl.BlockSpec(memory_space=pltpu.HBM)] * 3,
        out_specs=[pl.BlockSpec(memory_space=pltpu.VMEM)] * 4,
        scratch_shapes=[
            pltpu.VMEM(readings.shape, jnp.bfloat16),
            pltpu.VMEM(cell_ids.shape, jnp.int32),
            pltpu.SMEM(valid_days.shape, jnp.int32),
            pltpu.VMEM((devices, owned, width), jnp.bfloat16),
            pltpu.VMEM((devices, owned, width), jnp.bfloat16),
            pltpu.SemaphoreType.DMA((3,)),
            pltpu.SemaphoreType.DMA,
            pltpu.SemaphoreType.DMA,
            pltpu.SemaphoreType.DMA((QUARTERS,)),
            pltpu.SemaphoreType.REGULAR,
            pltpu.SemaphoreType.REGULAR,
        ],
        compiler_params=pltpu.CompilerParams(
            collective_id=0, has_side_effects=True, vmem_limit_bytes=40 * 1024 * 1024
        ),
        name="exchange",
    )(*[pltpu.with_memory_space_constraint(a, pltpu.HBM) for a in (readings, cell_ids, valid_days)])

    return pl.pallas_call(
        functools.partial(finish_kernel, days, features),
        out_shape=jax.ShapeDtypeStruct((owned, features * features), jnp.float32),
        in_specs=[pl.BlockSpec(memory_space=pltpu.VMEM)] * 4,
        out_specs=pl.BlockSpec(memory_space=pl.ANY),
        scratch_shapes=[
            pltpu.VMEM((pl.cdiv(features, LANES), owned * (features + SKEW), LANES), jnp.float32),
            pltpu.VMEM((owned, features * features), jnp.float32),
            pltpu.SemaphoreType.DMA((5,)),
        ],
        compiler_params=pltpu.CompilerParams(vmem_limit_bytes=24 * 1024 * 1024),
        name="finish",
    )(*[pltpu.with_memory_space_constraint(part, pltpu.VMEM) for part in parts])


def solution(mesh):
    return jax.shard_map(
        on_device,
        mesh=mesh,
        in_specs=(P(("cell", "tm"), None, None), P(("cell", "tm"), None), P()),
        out_specs=P(("cell", "tm"), None),
        check_vma=False,
    )
```

```python
import functools

import jax
import jax.numpy as jnp
from jax import lax
from jax.experimental import pallas as pl
from jax.experimental.pallas import tpu as pltpu
from jax.sharding import PartitionSpec as P

LANES = 128
SKEW = 1
QUARTERS = 4
NT = (((1,), (1,)), ((), ()))


def kernel(
    cells_axis, tm_devices, readings_ref, ids_ref, valid_in_ref, anomaly_ref, weight_ref, mean_ref, scale_ref,
    staged_ref, here_ref, valid_ref, ordered_ref, received_ref,
    load_sem, local_sem, send_sem, recv_sem, late_sem, go_sem,
):
    devices = cells_axis * tm_devices
    span = tm_devices // QUARTERS
    plane = devices // QUARTERS
    my_cell = lax.axis_index("cell")
    my_tm = lax.axis_index("tm")
    me = my_cell * tm_devices + my_tm
    quarter = my_tm // span
    low = my_tm % span
    early = quarter < 2

    def place_of(to_quarter, step):
        to_cell = lax.rem(my_cell + step // span, cells_axis)
        to_tm = to_quarter * span + lax.rem(low + step % span, span)
        return to_cell * tm_devices + to_tm, {"cell": to_cell, "tm": to_tm}

    def signal_plane(sem, to_quarter, first=0):
        def one(step, carry):
            _, place = place_of(to_quarter, step)
            pl.semaphore_signal(sem, inc=1, device_id=place, device_id_type=pl.DeviceIdType.MESH)
            return carry

        lax.fori_loop(first, plane, one, 0, unroll=True if plane <= 8 else 1)

    load = pltpu.make_async_copy(readings_ref, staged_ref, load_sem.at[0])
    load.start()
    load_ids = pltpu.make_async_copy(ids_ref, here_ref, load_sem.at[1])
    load_ids.start()
    load_valid = pltpu.make_async_copy(valid_in_ref, valid_ref, load_sem.at[2])
    load_valid.start()
    barrier = pltpu.get_barrier_semaphore()

    @pl.when(early)
    def _():
        signal_plane(barrier, 2)
        signal_plane(barrier, 3)
        signal_plane(barrier, 1 - quarter)
        signal_plane(barrier, quarter, 1)

    @pl.when(jnp.logical_not(early))
    def _():
        signal_plane(barrier, 0)

    @pl.when(quarter == 2)
    def _():
        signal_plane(barrier, 1)

    load_ids.wait()
    load.wait()
    days, features, cells = readings_ref.shape
    owned = cells // devices
    main = features // LANES * LANES
    rest = features - main
    pieces = [staged_ref[d, :main, :] for d in range(days)]
    if rest:
        pieces += [staged_ref[d, main:, :] for d in range(days)]
    columns = jnp.concatenate(pieces, axis=0)
    ids = here_ref[...]
    block = min(cells, 256)
    for start in range(0, cells, block):
        cell = lax.broadcasted_iota(jnp.int32, (block, cells), 0) + start
        pick = jnp.where(cell == ids, 1.0, 0.0).astype(jnp.bfloat16)
        ordered = lax.dot_general(pick, columns, NT, preferred_element_type=jnp.float32)
        ordered_ref[start // owned : (start + block) // owned] = ordered.reshape(
            block // owned, owned, days * features
        ).astype(jnp.bfloat16)

    own = pltpu.make_async_copy(ordered_ref.at[me], received_ref.at[me], local_sem)
    own.start()

    def send(to_quarter, step):
        index, place = place_of(to_quarter, step)
        pltpu.make_async_remote_copy(
            src_ref=ordered_ref.at[index],
            dst_ref=received_ref.at[me],
            send_sem=send_sem,
            recv_sem=recv_sem.at[quarter],
            device_id=place,
            device_id_type=pl.DeviceIdType.MESH,
        ).start()

    def send_planes(parts, first=0, last=plane):
        def one(step, carry):
            for to_quarter in parts:
                send(to_quarter, step)
            return carry

        lax.fori_loop(first, last, one, 0)

    def send_own():
        def one(step, carry):
            send(quarter, step)
            return carry

        lax.fori_loop(1, plane, one, 0)

    def signal_go(to_quarter):
        place = {"cell": my_cell, "tm": to_quarter * span + low}
        pl.semaphore_signal(go_sem, inc=1, device_id=place, device_id_type=pl.DeviceIdType.MESH)

    @pl.when(quarter == 0)
    def _():
        pl.semaphore_wait(barrier, devices - 1)
        send_planes([3])
        send_planes([2, 1])
        send_own()

    @pl.when(quarter == 1)
    def _():
        pl.semaphore_wait(barrier, 3 * plane - 1)
        send_planes([2, 0])
        send_own()
        pl.semaphore_wait(late_sem, plane)
        signal_go(2)
        signal_go(3)
        send_planes([3])

    @pl.when(quarter == 2)
    def _():
        pl.semaphore_wait(barrier, 2 * plane)
        send_planes([0])
        send_planes([1])
        pl.semaphore_wait(go_sem, 1)
        send_planes([3])
        send_own()

    @pl.when(quarter == 3)
    def _():
        pl.semaphore_wait(barrier, 2 * plane)
        signal_plane(late_sem, 1)
        send_planes([0])
        send_planes([1], plane * 0 // 8, plane * 3 // 8)
        pl.semaphore_wait(go_sem, 1)
        send_planes([1], plane * 3 // 8, plane * 8 // 8)
        send_planes([2])
        send_own()

    load_valid.wait()

    def arrive(source):
        @pl.when(source == quarter)
        def _():
            own.wait()
            less = pl.ds(0, plane - 1)
            pltpu.make_async_copy(
                received_ref.at[less], received_ref.at[less], recv_sem.at[source]
            ).wait()

        @pl.when(source != quarter)
        def _():
            every = pl.ds(0, plane)
            pltpu.make_async_copy(
                received_ref.at[every], received_ref.at[every], recv_sem.at[source]
            ).wait()

    order = range(QUARTERS)
    spread_all(
        days, features, span, arrive, order, valid_ref, received_ref, anomaly_ref, weight_ref, mean_ref,
        scale_ref,
    )
    others = pl.ds(0, devices - 1)
    pltpu.make_async_copy(ordered_ref.at[others], ordered_ref.at[others], send_sem).wait()


def spread_all(
    days, features, span, arrive, order, valid_ref, received_ref, anomaly_ref, weight_ref, mean_ref,
    scale_ref,
):
    slabs, owned, width = received_ref.shape
    main = features // LANES * LANES
    rest = features - main

    lane = lax.broadcasted_iota(jnp.int32, (owned, width), 1)
    day = lane // main if main else lane // rest
    if main and rest:
        day = jnp.where(lane < days * main, day, (lane - days * main) // rest)

    def weigh(slab, count):
        valid = valid_ref[slab]
        for d in range(days):
            weight_ref[d, pl.ds(slab, 1), :] = jnp.full((1, LANES), d < valid).astype(jnp.float32)
        return count + valid

    count = lax.fori_loop(0, slabs, weigh, jnp.int32(0), unroll=8)
    count = jnp.full((1, 1), count, jnp.int32).astype(jnp.float32)

    plane = slabs // QUARTERS
    apart = slabs // (plane // span)
    total = jnp.zeros((owned, width), jnp.float32)
    for source in order:
        arrive(source)

        for run in range(plane // span):
            first = run * apart + source * span

            def spread(slab, total):
                value = received_ref[slab].astype(jnp.float32)
                value = jnp.where(day < valid_ref[slab], value, 0.0)
                row = slab * (owned + SKEW)
                for tile in range(days * main // LANES):
                    piece = value[:, tile * LANES : (tile + 1) * LANES]
                    anomaly_ref[tile, pl.ds(row, owned), :] = piece
                if rest:
                    for d in range(days):
                        at = days * main + d * rest
                        tile = days * main // LANES + d
                        anomaly_ref[tile, pl.ds(row, owned), :rest] = value[:, at : at + rest]
                return total + value

            total = lax.fori_loop(first, first + span, spread, total, unroll=True)

    parts = []
    for start, size in ((0, main), (days * main, rest)):
        if size:
            part = total[:, start : start + size]
            for d in range(1, days):
                part = part + total[:, start + d * size : start + (d + 1) * size]
            parts.append(part / count)
    mean_ref[...] = jnp.concatenate(parts, axis=1)
    scale_ref[...] = jnp.broadcast_to(1.0 / (count - 1.0), scale_ref.shape)


def finish_kernel(
    days, features, anomaly_ref, weight_ref, mean_ref, scale_ref, out_ref,
    square_ref, laid_ref, out_sem,
):
    _, slabs, _ = weight_ref.shape
    owned = out_ref.shape[0]
    main = features // LANES * LANES
    scale = scale_ref[:1, :1]

    def turn(cell):
        by_day = []
        for d in range(days):
            part = []
            for tile in range(pl.cdiv(features, LANES)):
                at = tile * LANES
                size = min(LANES, features - at)
                index = d * (main // LANES) + tile if size == LANES else days * main // LANES + d
                rows = anomaly_ref[index, pl.ds(cell, slabs, stride=owned + SKEW), :]
                part.append(rows[:, :size] - weight_ref[d, :, :size] * mean_ref[cell : cell + 1, at : at + size])
            by_day.append(jnp.concatenate(part, axis=1))
        natural = jnp.concatenate(by_day, axis=0)
        flat = natural.astype(jnp.bfloat16)
        less = (natural - flat.astype(jnp.float32)).astype(jnp.bfloat16)
        turned = natural.T
        high = turned.astype(jnp.bfloat16)
        low = (turned - high.astype(jnp.float32)).astype(jnp.bfloat16)
        return high, low, flat, less

    def multiply(cell, high, low, flat, less):
        square = jnp.dot(
            jnp.concatenate([high, high, low], axis=1),
            jnp.concatenate([flat, less, flat], axis=0),
            preferred_element_type=jnp.float32,
        )
        square = square * scale
        at = cell * (features + SKEW)
        for tile, start in enumerate(range(0, features, LANES)):
            size = min(LANES, features - start)
            square_ref[tile, at : at + features, :size] = square[:, start : start + size]

    group = 4
    chunks = out_sem.shape[0]
    steps = features // group // chunks

    def lay_out(step, carry):
        first = step * group
        lines = []
        for i in range(group):
            for tile, start in enumerate(range(0, features, LANES)):
                line = square_ref[tile, pl.ds(first + i, owned, stride=features + SKEW), :]
                lines.append(line[:, : min(LANES, features - start)])
        at = pl.multiple_of(first * features, group * features)
        laid_ref[:, pl.ds(at, group * features)] = jnp.concatenate(lines, axis=1)
        return carry

    copies = []

    def give(chunk):
        lax.fori_loop(chunk * steps, (chunk + 1) * steps, lay_out, 0, unroll=True)
        size = steps * group * features
        at = pl.ds(chunk * size, size)
        copies.append(
            pltpu.make_async_copy(laid_ref.at[:, at], out_ref.at[:, at], out_sem.at[chunk])
        )
        copies[-1].start()

    for cell in range(owned):
        multiply(cell, *turn(cell))
    for chunk in range(chunks):
        give(chunk)
    for copy in copies:
        copy.wait()


def on_device(readings, cell_ids, valid_days):
    tm_devices = lax.axis_size("tm")
    cells_axis = lax.axis_size("cell")
    devices = cells_axis * tm_devices
    days, features, cells = readings.shape
    owned = cells // devices
    width = days * features
    tiles = days * pl.cdiv(features, LANES)
    parts = pl.pallas_call(
        functools.partial(kernel, cells_axis, tm_devices),
        out_shape=(
            pltpu.VMEM((tiles, devices * (owned + SKEW), LANES), jnp.float32),
            pltpu.VMEM((days, devices, LANES), jnp.float32),
            pltpu.VMEM((owned, features), jnp.float32),
            pltpu.VMEM((owned, LANES), jnp.float32),
        ),
        in_specs=[pl.BlockSpec(memory_space=pltpu.HBM)] * 3,
        out_specs=[pl.BlockSpec(memory_space=pltpu.VMEM)] * 4,
        scratch_shapes=[
            pltpu.VMEM(readings.shape, jnp.bfloat16),
            pltpu.VMEM(cell_ids.shape, jnp.int32),
            pltpu.SMEM(valid_days.shape, jnp.int32),
            pltpu.VMEM((devices, owned, width), jnp.bfloat16),
            pltpu.VMEM((devices, owned, width), jnp.bfloat16),
            pltpu.SemaphoreType.DMA((3,)),
            pltpu.SemaphoreType.DMA,
            pltpu.SemaphoreType.DMA,
            pltpu.SemaphoreType.DMA((QUARTERS,)),
            pltpu.SemaphoreType.REGULAR,
            pltpu.SemaphoreType.REGULAR,
        ],
        compiler_params=pltpu.CompilerParams(
            collective_id=0, has_side_effects=True, vmem_limit_bytes=40 * 1024 * 1024
        ),
        name="exchange",
    )(*[pltpu.with_memory_space_constraint(a, pltpu.HBM) for a in (readings, cell_ids, valid_days)])

    return pl.pallas_call(
        functools.partial(finish_kernel, days, features),
        out_shape=jax.ShapeDtypeStruct((owned, features * features), jnp.float32),
        in_specs=[pl.BlockSpec(memory_space=pltpu.VMEM)] * 4,
        out_specs=pl.BlockSpec(memory_space=pl.ANY),
        scratch_shapes=[
            pltpu.VMEM((pl.cdiv(features, LANES), owned * (features + SKEW), LANES), jnp.float32),
            pltpu.VMEM((owned, features * features), jnp.float32),
            pltpu.SemaphoreType.DMA((5,)),
        ],
        compiler_params=pltpu.CompilerParams(vmem_limit_bytes=24 * 1024 * 1024),
        name="finish",
    )(*[pltpu.with_memory_space_constraint(part, pltpu.VMEM) for part in parts])


def solution(mesh):
    return jax.shard_map(
        on_device,
        mesh=mesh,
        in_specs=(P(("cell", "tm"), None, None), P(("cell", "tm"), None), P()),
        out_specs=P(("cell", "tm"), None),
        check_vma=False,
    )
```

```python
import functools

import jax
import jax.numpy as jnp
from jax import lax
from jax.experimental import pallas as pl
from jax.experimental.pallas import tpu as pltpu
from jax.sharding import PartitionSpec as P

LANES = 128
SKEW = 1
QUARTERS = 4
NT = (((1,), (1,)), ((), ()))


def kernel(
    cells_axis, tm_devices, readings_ref, ids_ref, valid_in_ref, anomaly_ref, weight_ref, mean_ref, scale_ref,
    staged_ref, here_ref, valid_ref, ordered_ref, received_ref,
    load_sem, local_sem, send_sem, recv_sem, late_sem, go_sem,
):
    devices = cells_axis * tm_devices
    span = tm_devices // QUARTERS
    plane = devices // QUARTERS
    my_cell = lax.axis_index("cell")
    my_tm = lax.axis_index("tm")
    me = my_cell * tm_devices + my_tm
    quarter = my_tm // span
    low = my_tm % span
    early = quarter < 2

    def place_of(to_quarter, step):
        to_cell = lax.rem(my_cell + step // span, cells_axis)
        to_tm = to_quarter * span + lax.rem(low + step % span, span)
        return to_cell * tm_devices + to_tm, {"cell": to_cell, "tm": to_tm}

    def signal_plane(sem, to_quarter, first=0):
        def one(step, carry):
            _, place = place_of(to_quarter, step)
            pl.semaphore_signal(sem, inc=1, device_id=place, device_id_type=pl.DeviceIdType.MESH)
            return carry

        lax.fori_loop(first, plane, one, 0, unroll=True if plane <= 8 else 1)

    load = pltpu.make_async_copy(readings_ref, staged_ref, load_sem.at[0])
    load.start()
    load_ids = pltpu.make_async_copy(ids_ref, here_ref, load_sem.at[1])
    load_ids.start()
    load_valid = pltpu.make_async_copy(valid_in_ref, valid_ref, load_sem.at[2])
    load_valid.start()
    barrier = pltpu.get_barrier_semaphore()

    @pl.when(early)
    def _():
        signal_plane(barrier, 2)
        signal_plane(barrier, 3)
        signal_plane(barrier, 1 - quarter)
        signal_plane(barrier, quarter, 1)

    @pl.when(jnp.logical_not(early))
    def _():
        signal_plane(barrier, 0)

    @pl.when(quarter == 2)
    def _():
        signal_plane(barrier, 1)

    load_ids.wait()
    load.wait()
    days, features, cells = readings_ref.shape
    owned = cells // devices
    main = features // LANES * LANES
    rest = features - main
    pieces = [staged_ref[d, :main, :] for d in range(days)]
    if rest:
        pieces += [staged_ref[d, main:, :] for d in range(days)]
    columns = jnp.concatenate(pieces, axis=0)
    ids = here_ref[...]
    block = min(cells, 256)
    for start in range(0, cells, block):
        cell = lax.broadcasted_iota(jnp.int32, (block, cells), 0) + start
        pick = jnp.where(cell == ids, 1.0, 0.0).astype(jnp.bfloat16)
        ordered = lax.dot_general(pick, columns, NT, preferred_element_type=jnp.float32)
        ordered_ref[start // owned : (start + block) // owned] = ordered.reshape(
            block // owned, owned, days * features
        ).astype(jnp.bfloat16)

    own = pltpu.make_async_copy(ordered_ref.at[me], received_ref.at[me], local_sem)
    own.start()

    def send(to_quarter, step):
        index, place = place_of(to_quarter, step)
        pltpu.make_async_remote_copy(
            src_ref=ordered_ref.at[index],
            dst_ref=received_ref.at[me],
            send_sem=send_sem,
            recv_sem=recv_sem.at[quarter],
            device_id=place,
            device_id_type=pl.DeviceIdType.MESH,
        ).start()

    def send_planes(parts, first=0, last=plane):
        def one(step, carry):
            for to_quarter in parts:
                send(to_quarter, step)
            return carry

        lax.fori_loop(first, last, one, 0)

    def send_own():
        def one(step, carry):
            send(quarter, step)
            return carry

        lax.fori_loop(1, plane, one, 0)

    def signal_go(to_quarter):
        place = {"cell": my_cell, "tm": to_quarter * span + low}
        pl.semaphore_signal(go_sem, inc=1, device_id=place, device_id_type=pl.DeviceIdType.MESH)

    @pl.when(quarter == 0)
    def _():
        pl.semaphore_wait(barrier, devices - 1)
        send_planes([3])
        send_planes([2, 1])
        send_own()

    @pl.when(quarter == 1)
    def _():
        pl.semaphore_wait(barrier, 3 * plane - 1)
        send_planes([2, 0])
        send_own()
        pl.semaphore_wait(late_sem, plane)
        signal_go(2)
        signal_go(3)
        send_planes([3])

    @pl.when(quarter == 2)
    def _():
        pl.semaphore_wait(barrier, 2 * plane)
        send_planes([0])
        send_planes([1])
        pl.semaphore_wait(go_sem, 1)
        send_planes([3])
        send_own()

    @pl.when(quarter == 3)
    def _():
        pl.semaphore_wait(barrier, 2 * plane)
        signal_plane(late_sem, 1)
        send_planes([0])
        send_planes([1], plane * 0 // 8, plane * 2 // 8)
        pl.semaphore_wait(go_sem, 1)
        send_planes([1], plane * 2 // 8, plane * 8 // 8)
        send_planes([2])
        send_own()

    load_valid.wait()

    def arrive(source):
        @pl.when(source == quarter)
        def _():
            own.wait()
            less = pl.ds(0, plane - 1)
            pltpu.make_async_copy(
                received_ref.at[less], received_ref.at[less], recv_sem.at[source]
            ).wait()

        @pl.when(source != quarter)
        def _():
            every = pl.ds(0, plane)
            pltpu.make_async_copy(
                received_ref.at[every], received_ref.at[every], recv_sem.at[source]
            ).wait()

    order = range(QUARTERS)
    spread_all(
        days, features, span, arrive, order, valid_ref, received_ref, anomaly_ref, weight_ref, mean_ref,
        scale_ref,
    )
    others = pl.ds(0, devices - 1)
    pltpu.make_async_copy(ordered_ref.at[others], ordered_ref.at[others], send_sem).wait()


def spread_all(
    days, features, span, arrive, order, valid_ref, received_ref, anomaly_ref, weight_ref, mean_ref,
    scale_ref,
):
    slabs, owned, width = received_ref.shape
    main = features // LANES * LANES
    rest = features - main

    lane = lax.broadcasted_iota(jnp.int32, (owned, width), 1)
    day = lane // main if main else lane // rest
    if main and rest:
        day = jnp.where(lane < days * main, day, (lane - days * main) // rest)

    def weigh(slab, count):
        valid = valid_ref[slab]
        for d in range(days):
            weight_ref[d, pl.ds(slab, 1), :] = jnp.full((1, LANES), d < valid).astype(jnp.float32)
        return count + valid

    count = lax.fori_loop(0, slabs, weigh, jnp.int32(0), unroll=8)
    count = jnp.full((1, 1), count, jnp.int32).astype(jnp.float32)

    plane = slabs // QUARTERS
    apart = slabs // (plane // span)
    total = jnp.zeros((owned, width), jnp.float32)
    for source in order:
        arrive(source)

        for run in range(plane // span):
            first = run * apart + source * span

            def spread(slab, total):
                value = received_ref[slab].astype(jnp.float32)
                value = jnp.where(day < valid_ref[slab], value, 0.0)
                row = slab * (owned + SKEW)
                for tile in range(days * main // LANES):
                    piece = value[:, tile * LANES : (tile + 1) * LANES]
                    anomaly_ref[tile, pl.ds(row, owned), :] = piece
                if rest:
                    for d in range(days):
                        at = days * main + d * rest
                        tile = days * main // LANES + d
                        anomaly_ref[tile, pl.ds(row, owned), :rest] = value[:, at : at + rest]
                return total + value

            total = lax.fori_loop(first, first + span, spread, total, unroll=True)

    parts = []
    for start, size in ((0, main), (days * main, rest)):
        if size:
            part = total[:, start : start + size]
            for d in range(1, days):
                part = part + total[:, start + d * size : start + (d + 1) * size]
            parts.append(part / count)
    mean_ref[...] = jnp.concatenate(parts, axis=1)
    scale_ref[...] = jnp.broadcast_to(1.0 / (count - 1.0), scale_ref.shape)


def finish_kernel(
    days, features, anomaly_ref, weight_ref, mean_ref, scale_ref, out_ref,
    square_ref, laid_ref, out_sem,
):
    _, slabs, _ = weight_ref.shape
    owned = out_ref.shape[0]
    main = features // LANES * LANES
    scale = scale_ref[:1, :1]

    def turn(cell):
        by_day = []
        for d in range(days):
            part = []
            for tile in range(pl.cdiv(features, LANES)):
                at = tile * LANES
                size = min(LANES, features - at)
                index = d * (main // LANES) + tile if size == LANES else days * main // LANES + d
                rows = anomaly_ref[index, pl.ds(cell, slabs, stride=owned + SKEW), :]
                part.append(rows[:, :size] - weight_ref[d, :, :size] * mean_ref[cell : cell + 1, at : at + size])
            by_day.append(jnp.concatenate(part, axis=1))
        natural = jnp.concatenate(by_day, axis=0)
        flat = natural.astype(jnp.bfloat16)
        less = (natural - flat.astype(jnp.float32)).astype(jnp.bfloat16)
        turned = natural.T
        high = turned.astype(jnp.bfloat16)
        low = (turned - high.astype(jnp.float32)).astype(jnp.bfloat16)
        return high, low, flat, less

    def multiply(cell, high, low, flat, less):
        square = jnp.dot(
            jnp.concatenate([high, high, low], axis=1),
            jnp.concatenate([flat, less, flat], axis=0),
            preferred_element_type=jnp.float32,
        )
        square = square * scale
        at = cell * (features + SKEW)
        for tile, start in enumerate(range(0, features, LANES)):
            size = min(LANES, features - start)
            square_ref[tile, at : at + features, :size] = square[:, start : start + size]

    group = 4
    chunks = out_sem.shape[0]
    steps = features // group // chunks

    def lay_out(step, carry):
        first = step * group
        lines = []
        for i in range(group):
            for tile, start in enumerate(range(0, features, LANES)):
                line = square_ref[tile, pl.ds(first + i, owned, stride=features + SKEW), :]
                lines.append(line[:, : min(LANES, features - start)])
        at = pl.multiple_of(first * features, group * features)
        laid_ref[:, pl.ds(at, group * features)] = jnp.concatenate(lines, axis=1)
        return carry

    copies = []

    def give(chunk):
        lax.fori_loop(chunk * steps, (chunk + 1) * steps, lay_out, 0, unroll=True)
        size = steps * group * features
        at = pl.ds(chunk * size, size)
        copies.append(
            pltpu.make_async_copy(laid_ref.at[:, at], out_ref.at[:, at], out_sem.at[chunk])
        )
        copies[-1].start()

    for cell in range(owned):
        multiply(cell, *turn(cell))
    for chunk in range(chunks):
        give(chunk)
    for copy in copies:
        copy.wait()


def on_device(readings, cell_ids, valid_days):
    tm_devices = lax.axis_size("tm")
    cells_axis = lax.axis_size("cell")
    devices = cells_axis * tm_devices
    days, features, cells = readings.shape
    owned = cells // devices
    width = days * features
    tiles = days * pl.cdiv(features, LANES)
    parts = pl.pallas_call(
        functools.partial(kernel, cells_axis, tm_devices),
        out_shape=(
            pltpu.VMEM((tiles, devices * (owned + SKEW), LANES), jnp.float32),
            pltpu.VMEM((days, devices, LANES), jnp.float32),
            pltpu.VMEM((owned, features), jnp.float32),
            pltpu.VMEM((owned, LANES), jnp.float32),
        ),
        in_specs=[pl.BlockSpec(memory_space=pltpu.HBM)] * 3,
        out_specs=[pl.BlockSpec(memory_space=pltpu.VMEM)] * 4,
        scratch_shapes=[
            pltpu.VMEM(readings.shape, jnp.bfloat16),
            pltpu.VMEM(cell_ids.shape, jnp.int32),
            pltpu.SMEM(valid_days.shape, jnp.int32),
            pltpu.VMEM((devices, owned, width), jnp.bfloat16),
            pltpu.VMEM((devices, owned, width), jnp.bfloat16),
            pltpu.SemaphoreType.DMA((3,)),
            pltpu.SemaphoreType.DMA,
            pltpu.SemaphoreType.DMA,
            pltpu.SemaphoreType.DMA((QUARTERS,)),
            pltpu.SemaphoreType.REGULAR,
            pltpu.SemaphoreType.REGULAR,
        ],
        compiler_params=pltpu.CompilerParams(
            collective_id=0, has_side_effects=True, vmem_limit_bytes=40 * 1024 * 1024
        ),
        name="exchange",
    )(*[pltpu.with_memory_space_constraint(a, pltpu.HBM) for a in (readings, cell_ids, valid_days)])

    return pl.pallas_call(
        functools.partial(finish_kernel, days, features),
        out_shape=jax.ShapeDtypeStruct((owned, features * features), jnp.float32),
        in_specs=[pl.BlockSpec(memory_space=pltpu.VMEM)] * 4,
        out_specs=pl.BlockSpec(memory_space=pl.ANY),
        scratch_shapes=[
            pltpu.VMEM((pl.cdiv(features, LANES), owned * (features + SKEW), LANES), jnp.float32),
            pltpu.VMEM((owned, features * features), jnp.float32),
            pltpu.SemaphoreType.DMA((5,)),
        ],
        compiler_params=pltpu.CompilerParams(vmem_limit_bytes=24 * 1024 * 1024),
        name="finish",
    )(*[pltpu.with_memory_space_constraint(part, pltpu.VMEM) for part in parts])


def solution(mesh):
    return jax.shard_map(
        on_device,
        mesh=mesh,
        in_specs=(P(("cell", "tm"), None, None), P(("cell", "tm"), None), P()),
        out_specs=P(("cell", "tm"), None),
        check_vma=False,
    )
```

```python
import functools

import jax
import jax.numpy as jnp
from jax import lax
from jax.experimental import pallas as pl
from jax.experimental.pallas import tpu as pltpu
from jax.sharding import PartitionSpec as P

LANES = 128
SKEW = 1
QUARTERS = 4
NT = (((1,), (1,)), ((), ()))


def kernel(
    cells_axis, tm_devices, readings_ref, ids_ref, valid_in_ref, anomaly_ref, weight_ref, mean_ref, scale_ref,
    staged_ref, here_ref, valid_ref, ordered_ref, received_ref,
    load_sem, local_sem, send_sem, recv_sem, late_sem, go_sem,
):
    devices = cells_axis * tm_devices
    span = tm_devices // QUARTERS
    plane = devices // QUARTERS
    my_cell = lax.axis_index("cell")
    my_tm = lax.axis_index("tm")
    me = my_cell * tm_devices + my_tm
    quarter = my_tm // span
    low = my_tm % span
    early = quarter < 2

    def place_of(to_quarter, step):
        to_cell = lax.rem(my_cell + step // span, cells_axis)
        to_tm = to_quarter * span + lax.rem(low + step % span, span)
        return to_cell * tm_devices + to_tm, {"cell": to_cell, "tm": to_tm}

    def signal_plane(sem, to_quarter, first=0):
        def one(step, carry):
            _, place = place_of(to_quarter, step)
            pl.semaphore_signal(sem, inc=1, device_id=place, device_id_type=pl.DeviceIdType.MESH)
            return carry

        lax.fori_loop(first, plane, one, 0, unroll=True if plane <= 8 else 1)

    load = pltpu.make_async_copy(readings_ref, staged_ref, load_sem.at[0])
    load.start()
    load_ids = pltpu.make_async_copy(ids_ref, here_ref, load_sem.at[1])
    load_ids.start()
    load_valid = pltpu.make_async_copy(valid_in_ref, valid_ref, load_sem.at[2])
    load_valid.start()
    barrier = pltpu.get_barrier_semaphore()

    @pl.when(early)
    def _():
        signal_plane(barrier, 2)
        signal_plane(barrier, 3)
        signal_plane(barrier, 1 - quarter)
        signal_plane(barrier, quarter, 1)

    @pl.when(jnp.logical_not(early))
    def _():
        signal_plane(barrier, 0)

    @pl.when(quarter == 2)
    def _():
        signal_plane(barrier, 1)

    load_ids.wait()
    load.wait()
    days, features, cells = readings_ref.shape
    owned = cells // devices
    main = features // LANES * LANES
    rest = features - main
    pieces = [staged_ref[d, :main, :] for d in range(days)]
    if rest:
        pieces += [staged_ref[d, main:, :] for d in range(days)]
    columns = jnp.concatenate(pieces, axis=0)
    ids = here_ref[...]
    block = min(cells, 256)
    for start in range(0, cells, block):
        cell = lax.broadcasted_iota(jnp.int32, (block, cells), 0) + start
        pick = jnp.where(cell == ids, 1.0, 0.0).astype(jnp.bfloat16)
        ordered = lax.dot_general(pick, columns, NT, preferred_element_type=jnp.float32)
        ordered_ref[start // owned : (start + block) // owned] = ordered.reshape(
            block // owned, owned, days * features
        ).astype(jnp.bfloat16)

    own = pltpu.make_async_copy(ordered_ref.at[me], received_ref.at[me], local_sem)
    own.start()

    def send(to_quarter, step):
        index, place = place_of(to_quarter, step)
        pltpu.make_async_remote_copy(
            src_ref=ordered_ref.at[index],
            dst_ref=received_ref.at[me],
            send_sem=send_sem,
            recv_sem=recv_sem.at[quarter],
            device_id=place,
            device_id_type=pl.DeviceIdType.MESH,
        ).start()

    def send_planes(parts, first=0, last=plane):
        def one(step, carry):
            for to_quarter in parts:
                send(to_quarter, step)
            return carry

        lax.fori_loop(first, last, one, 0)

    def send_own():
        def one(step, carry):
            send(quarter, step)
            return carry

        lax.fori_loop(1, plane, one, 0)

    def signal_go(to_quarter):
        place = {"cell": my_cell, "tm": to_quarter * span + low}
        pl.semaphore_signal(go_sem, inc=1, device_id=place, device_id_type=pl.DeviceIdType.MESH)

    @pl.when(quarter == 0)
    def _():
        pl.semaphore_wait(barrier, devices - 1)
        send_planes([3])
        send_planes([2, 1])
        send_own()

    @pl.when(quarter == 1)
    def _():
        pl.semaphore_wait(barrier, 3 * plane - 1)
        send_planes([2, 0])
        send_own()
        pl.semaphore_wait(late_sem, plane)
        signal_go(2)
        signal_go(3)
        send_planes([3])

    @pl.when(quarter == 2)
    def _():
        pl.semaphore_wait(barrier, 2 * plane)
        send_planes([0])
        send_planes([1])
        pl.semaphore_wait(go_sem, 1)
        send_planes([3])
        send_own()

    @pl.when(quarter == 3)
    def _():
        pl.semaphore_wait(barrier, 2 * plane)
        signal_plane(late_sem, 1)
        send_planes([0])
        send_planes([1], plane * 0 // 8, plane * 2 // 8)
        pl.semaphore_wait(go_sem, 1)
        send_planes([1], plane * 2 // 8, plane * 8 // 8)
        send_planes([2])
        send_own()

    load_valid.wait()

    def arrive(source):
        @pl.when(source == quarter)
        def _():
            own.wait()
            less = pl.ds(0, plane - 1)
            pltpu.make_async_copy(
                received_ref.at[less], received_ref.at[less], recv_sem.at[source]
            ).wait()

        @pl.when(source != quarter)
        def _():
            every = pl.ds(0, plane)
            pltpu.make_async_copy(
                received_ref.at[every], received_ref.at[every], recv_sem.at[source]
            ).wait()

    order = range(QUARTERS)
    spread_all(
        days, features, span, arrive, order, valid_ref, received_ref, anomaly_ref, weight_ref, mean_ref,
        scale_ref,
    )
    others = pl.ds(0, devices - 1)
    pltpu.make_async_copy(ordered_ref.at[others], ordered_ref.at[others], send_sem).wait()


def spread_all(
    days, features, span, arrive, order, valid_ref, received_ref, anomaly_ref, weight_ref, mean_ref,
    scale_ref,
):
    slabs, owned, width = received_ref.shape
    main = features // LANES * LANES
    rest = features - main

    lane = lax.broadcasted_iota(jnp.int32, (owned, width), 1)
    day = lane // main if main else lane // rest
    if main and rest:
        day = jnp.where(lane < days * main, day, (lane - days * main) // rest)

    def weigh(slab, count):
        valid = valid_ref[slab]
        for d in range(days):
            weight_ref[d, pl.ds(slab, 1), :] = jnp.full((1, LANES), d < valid).astype(jnp.float32)
        return count + valid

    count = lax.fori_loop(0, slabs, weigh, jnp.int32(0), unroll=8)
    count = jnp.full((1, 1), count, jnp.int32).astype(jnp.float32)

    plane = slabs // QUARTERS
    apart = slabs // (plane // span)
    total = jnp.zeros((owned, width), jnp.float32)
    for source in order:
        arrive(source)

        for run in range(plane // span):
            first = run * apart + source * span

            def spread(slab, total):
                value = received_ref[slab].astype(jnp.float32)
                value = jnp.where(day < valid_ref[slab], value, 0.0)
                row = slab * (owned + SKEW)
                for tile in range(days * main // LANES):
                    piece = value[:, tile * LANES : (tile + 1) * LANES]
                    anomaly_ref[tile, pl.ds(row, owned), :] = piece
                if rest:
                    for d in range(days):
                        at = days * main + d * rest
                        tile = days * main // LANES + d
                        anomaly_ref[tile, pl.ds(row, owned), :rest] = value[:, at : at + rest]
                return total + value

            total = lax.fori_loop(first, first + span, spread, total, unroll=True)

    parts = []
    for start, size in ((0, main), (days * main, rest)):
        if size:
            part = total[:, start : start + size]
            for d in range(1, days):
                part = part + total[:, start + d * size : start + (d + 1) * size]
            parts.append(part / count)
    mean_ref[...] = jnp.concatenate(parts, axis=1)
    scale_ref[...] = jnp.broadcast_to(1.0 / (count - 1.0), scale_ref.shape)


def finish_kernel(
    days, features, anomaly_ref, weight_ref, mean_ref, scale_ref, out_ref,
    square_ref, laid_ref, out_sem,
):
    _, slabs, _ = weight_ref.shape
    owned = out_ref.shape[0]
    main = features // LANES * LANES
    scale = scale_ref[:1, :1]

    def turn(cell):
        by_day = []
        for d in range(days):
            part = []
            for tile in range(pl.cdiv(features, LANES)):
                at = tile * LANES
                size = min(LANES, features - at)
                index = d * (main // LANES) + tile if size == LANES else days * main // LANES + d
                rows = anomaly_ref[index, pl.ds(cell, slabs, stride=owned + SKEW), :]
                part.append(rows[:, :size] - weight_ref[d, :, :size] * mean_ref[cell : cell + 1, at : at + size])
            by_day.append(jnp.concatenate(part, axis=1))
        natural = jnp.concatenate(by_day, axis=0)
        flat = natural.astype(jnp.bfloat16)
        less = (natural - flat.astype(jnp.float32)).astype(jnp.bfloat16)
        turned = natural.T * scale
        high = turned.astype(jnp.bfloat16)
        low = (turned - high.astype(jnp.float32)).astype(jnp.bfloat16)
        return high, low, flat, less

    def multiply(cell, high, low, flat, less):
        square = jnp.dot(
            jnp.concatenate([high, high, low], axis=1),
            jnp.concatenate([flat, less, flat], axis=0),
            preferred_element_type=jnp.float32,
        )
        at = cell * (features + SKEW)
        for tile, start in enumerate(range(0, features, LANES)):
            size = min(LANES, features - start)
            square_ref[tile, at : at + features, :size] = square[:, start : start + size]

    group = 4
    chunks = out_sem.shape[0]
    steps = features // group // chunks

    def lay_out(step, carry):
        first = step * group
        lines = []
        for i in range(group):
            for tile, start in enumerate(range(0, features, LANES)):
                line = square_ref[tile, pl.ds(first + i, owned, stride=features + SKEW), :]
                lines.append(line[:, : min(LANES, features - start)])
        at = pl.multiple_of(first * features, group * features)
        laid_ref[:, pl.ds(at, group * features)] = jnp.concatenate(lines, axis=1)
        return carry

    copies = []

    def give(chunk):
        lax.fori_loop(chunk * steps, (chunk + 1) * steps, lay_out, 0, unroll=True)
        size = steps * group * features
        at = pl.ds(chunk * size, size)
        copies.append(
            pltpu.make_async_copy(laid_ref.at[:, at], out_ref.at[:, at], out_sem.at[chunk])
        )
        copies[-1].start()

    for cell in range(owned):
        multiply(cell, *turn(cell))
    for chunk in range(chunks):
        give(chunk)
    for copy in copies:
        copy.wait()


def on_device(readings, cell_ids, valid_days):
    tm_devices = lax.axis_size("tm")
    cells_axis = lax.axis_size("cell")
    devices = cells_axis * tm_devices
    days, features, cells = readings.shape
    owned = cells // devices
    width = days * features
    tiles = days * pl.cdiv(features, LANES)
    parts = pl.pallas_call(
        functools.partial(kernel, cells_axis, tm_devices),
        out_shape=(
            pltpu.VMEM((tiles, devices * (owned + SKEW), LANES), jnp.float32),
            pltpu.VMEM((days, devices, LANES), jnp.float32),
            pltpu.VMEM((owned, features), jnp.float32),
            pltpu.VMEM((owned, LANES), jnp.float32),
        ),
        in_specs=[pl.BlockSpec(memory_space=pltpu.HBM)] * 3,
        out_specs=[pl.BlockSpec(memory_space=pltpu.VMEM)] * 4,
        scratch_shapes=[
            pltpu.VMEM(readings.shape, jnp.bfloat16),
            pltpu.VMEM(cell_ids.shape, jnp.int32),
            pltpu.SMEM(valid_days.shape, jnp.int32),
            pltpu.VMEM((devices, owned, width), jnp.bfloat16),
            pltpu.VMEM((devices, owned, width), jnp.bfloat16),
            pltpu.SemaphoreType.DMA((3,)),
            pltpu.SemaphoreType.DMA,
            pltpu.SemaphoreType.DMA,
            pltpu.SemaphoreType.DMA((QUARTERS,)),
            pltpu.SemaphoreType.REGULAR,
            pltpu.SemaphoreType.REGULAR,
        ],
        compiler_params=pltpu.CompilerParams(
            collective_id=0, has_side_effects=True, vmem_limit_bytes=40 * 1024 * 1024
        ),
        name="exchange",
    )(*[pltpu.with_memory_space_constraint(a, pltpu.HBM) for a in (readings, cell_ids, valid_days)])

    return pl.pallas_call(
        functools.partial(finish_kernel, days, features),
        out_shape=jax.ShapeDtypeStruct((owned, features * features), jnp.float32),
        in_specs=[pl.BlockSpec(memory_space=pltpu.VMEM)] * 4,
        out_specs=pl.BlockSpec(memory_space=pl.ANY),
        scratch_shapes=[
            pltpu.VMEM((pl.cdiv(features, LANES), owned * (features + SKEW), LANES), jnp.float32),
            pltpu.VMEM((owned, features * features), jnp.float32),
            pltpu.SemaphoreType.DMA((5,)),
        ],
        compiler_params=pltpu.CompilerParams(vmem_limit_bytes=24 * 1024 * 1024),
        name="finish",
    )(*[pltpu.with_memory_space_constraint(part, pltpu.VMEM) for part in parts])


def solution(mesh):
    return jax.shard_map(
        on_device,
        mesh=mesh,
        in_specs=(P(("cell", "tm"), None, None), P(("cell", "tm"), None), P()),
        out_specs=P(("cell", "tm"), None),
        check_vma=False,
    )
```
